512 devices in a mesh: sub: 64 (over z_lo, y, core), slab: 8 (over z_hi, x).
Axes of the slice: x: 4, y: 8, z: 8 (z_hi: 2, z_lo: 4; z = z_hi * 4 + z_lo), core: 2. Of those that a mesh axis runs over, the one named last changes fastest.
Arguments:
- source: float32 [4, 1048576], P(None, ('sub', 'slab')), may hold values from -6 to 6
- operator: float32 [7, 4, 4, 1048576], P(None, None, None, ('sub', 'slab')), as said below
- prolong: float32 [4, 4, 1048576], P(None, None, ('sub', 'slab')), may hold values from -2 to 2
- columns: int32 [7, 1048576], P(None, ('sub', 'slab')), may hold values from 0 to 4095, as said below
- slots: int32 [7, 1048576], P(None, ('sub', 'slab')), may hold values from 0 to 6
- aggregates: int32 [1048576], P(('sub', 'slab')), may hold values from 0 to 255, as said below
- sends: int32 [1048576], P(('sub', 'slab')), may hold values from 0 to 2047, as said below
- prolong_one: float32 [4, 4, 262144], P(None, None, ('sub', 'slab')), as said below
- columns_one: int32 [7, 262144], P(None, ('sub', 'slab')), may hold values from 0 to 895, as said below
- slots_one: int32 [7, 262144], P(None, ('sub', 'slab')), may hold values from 0 to 6, as said below
- aggregates_one: int32 [262144], P(('sub', 'slab')), may hold values from 0 to 63, as said below
- sends_one: int32 [196608], P(('sub', 'slab')), may hold values from 0 to 511, as said below
- columns_two: int32 [7, 65536], P(None, ('sub', 'slab')), may hold values from 0 to 287, as said below
- sends_two: int32 [81920], P(('sub', 'slab')), may hold values from 0 to 127, as said below
Outputs:
- smoothed: float32 [4, 1048576], P(None, ('sub', 'slab'))
- smoothed_one: float32 [4, 131072], P(None, ('sub', 'slab'))
- smoothed_two: float32 [4, 16384], P(None, ('sub', 'slab'))
The draws below stay inside these ranges and needn't reach their ends.
Inputs may be any that keep to these rules, and one draw needn't show every extreme that they name: Fine operator blocks; no other structure. `columns`: values below 2048 name the subdomain's own rows, the rest its ghost rows; every neighbour of a fine cell lies one or two cells away along one grid dimension, the third dimension closes into a loop. `aggregates`: eight fine rows a first-level aggregate. `sends`: local row numbers of the fine subdomain. `prolong_one`: equal on the two devices of a merged subdomain. `columns_one`: values below 512 name the merged subdomain's rows, the rest its ghost rows; equal on both devices of a merged subdomain. `slots_one`: equal on both devices of a merged subdomain. `aggregates_one`: eight first-level rows a second-level aggregate; equal on both devices of a merged subdomain. `sends_one`: row numbers of the merged first-level subdomain. `columns_two`: values below 128 name the merged subdomain's rows, the rest its ghost rows; equal on all four devices of a merged subdomain. `sends_two`: row numbers of the merged second-level subdomain.
All inputs are finite; a program needn't handle non-finite values.
Results may differ from the reference program's by a relative error of at most 0.0001.
Values sent between devices are 32-bit elements; how exact they have to be, the bound alone decides.
A program may use at most 128 MiB of HBM per device.

```python
from functools import partial
import jax
import jax.numpy as jnp
from jax import lax

GX = 8
GY = 8
GZ = 32
CELLS = 2048
N_SUB = 64
N_SLAB = 8
DEVICES = 512


DIRECTIONS = ((0, 0, 0), (-1, 0, 0), (1, 0, 0), (0, -1, 0), (0, 1, 0), (0, 0, -1), (0, 0, 1))


def level_shape(level):
    return (GX >> level, GY, GZ >> level, N_SUB >> level)


def exchange_values(values, first, second):
    return jnp.where(values == first, second, jnp.where(values == second, first, values))


def level_numbering(key, level):
    span_x, span_y, span_z, groups = level_shape(level)
    halves = 1 if level == 0 else 2
    half_y = span_y // halves
    half_cells = span_x * half_y * span_z
    subkeys = jax.random.split(jax.random.fold_in(key, 100 + level), groups * N_SLAB * halves)

    def permute(subkey):
        order = jax.random.permutation(subkey, half_cells).astype(jnp.int32)
        order = exchange_values(order, order[0], jnp.int32(0))
        order = exchange_values(order, order[half_cells - 1], jnp.int32(half_cells - 1))
        return order
    perms = jax.vmap(permute)(subkeys)
    perms = perms.reshape(groups, N_SLAB, halves, span_x, half_y, span_z)
    perms = perms + (jnp.arange(halves, dtype=jnp.int32) * half_cells).reshape(1, 1, halves, 1, 1, 1)
    return perms.transpose(0, 1, 3, 2, 4, 5).reshape(groups, N_SLAB, span_x, span_y, span_z)


def level_coords(level):
    span_x, span_y, span_z, groups = level_shape(level)
    shape = (groups, N_SLAB, span_x, span_y, span_z)
    return [lax.broadcasted_iota(jnp.int32, shape, axis) for axis in range(5)]


def level_links(number, level, distance):
    span_x, span_y, span_z, groups = level_shape(level)
    depth = 2 if level == 0 else 1
    cells = span_x * span_y * span_z
    first_count = depth * span_y * span_z
    second_count = span_x * depth * span_z
    group_id, slab_id, coord_x, coord_y, coord_z = level_coords(level)
    result = []
    for slot_index in range(7):
        dir_x, dir_y, dir_z = DIRECTIONS[slot_index]
        stride = distance[slot_index]
        near_x = coord_x + dir_x * stride
        near_y = coord_y + dir_y * stride
        near_z = (coord_z + dir_z * stride) % span_z
        clip_x = jnp.clip(near_x, 0, span_x - 1)
        clip_y = jnp.clip(near_y, 0, span_y - 1)
        local = number[group_id, slab_id, clip_x, clip_y, near_z]
        below_x = cells + ((near_x + depth) * span_y + near_y) * span_z + near_z
        above_x = cells + first_count + ((near_x - span_x) * span_y + near_y) * span_z + near_z
        below_y = cells + 2 * first_count + (near_x * depth + near_y + depth) * span_z + near_z
        above_y = cells + 2 * first_count + second_count + (near_x * depth + near_y - span_y) * span_z + near_z
        link = jnp.where(near_x < 0, below_x, jnp.where(near_x >= span_x, above_x, jnp.where(near_y < 0, below_y, jnp.where(near_y >= span_y, above_y, local))))
        result.append(link.astype(jnp.int32))
    return jnp.stack(result)


def level_slots(level, distance):
    span_x, span_y, span_z, groups = level_shape(level)
    group_id, slab_id, coord_x, coord_y, coord_z = level_coords(level)
    result = []
    for slot_index in range(7):
        dir_x, dir_y, dir_z = DIRECTIONS[slot_index]
        stride = distance[slot_index]
        same = ((coord_x + dir_x * stride) // 2 == coord_x // 2) & ((coord_y + dir_y * stride) // 2 == coord_y // 2)
        same = same & ((coord_z + dir_z * stride) % span_z // 2 == coord_z // 2)
        result.append(jnp.where(same, 0, slot_index).astype(jnp.int32))
    return jnp.stack(result)


def level_aggregates(level, next_number):
    span_x, span_y, span_z, groups = level_shape(level)
    group_id, slab_id, coord_x, coord_y, coord_z = level_coords(level)
    coarse_global = (group_id * span_y + coord_y) // 2
    coarse_group = coarse_global // span_y
    coarse_y = coarse_global % span_y
    index = next_number[coarse_group, slab_id, coord_x // 2, coarse_y, coord_z // 2]
    half_cells = span_x // 2 * span_y * (span_z // 2) // 2
    return (index - (coarse_y >= span_y // 2).astype(jnp.int32) * half_cells).astype(jnp.int32)


def level_sends(number, level):
    span_x, span_y, span_z, groups = level_shape(level)
    depth = 2 if level == 0 else 1
    low_first = number[:, :, :depth].reshape(groups, N_SLAB, -1)
    high_first = number[:, :, span_x - depth:].reshape(groups, N_SLAB, -1)
    low_second = number[:, :, :, :depth].reshape(groups, N_SLAB, -1)
    high_second = number[:, :, :, span_y - depth:].reshape(groups, N_SLAB, -1)
    return jnp.concatenate([low_first, high_first, low_second, high_second], axis=-1)


def by_index(values, number):
    lead = values.shape[:-5]
    groups = number.shape[0]
    flat_number = number.reshape(groups * N_SLAB, -1)
    flat_values = values.reshape((-1, groups * N_SLAB, flat_number.shape[1]))

    def place(entries, targets):
        return jnp.zeros_like(entries).at[:, targets].set(entries)
    placed = jax.vmap(place, in_axes=(1, 0), out_axes=1)(flat_values, flat_number)
    return placed.reshape(lead + (groups, N_SLAB, -1))


def spread(values, level):
    lead_count = values.ndim - 3
    repeated = jnp.repeat(values, 1 << level, axis=lead_count)
    return repeated.reshape(values.shape[:lead_count] + (-1,))


def hierarchy(key):
    number_zero = level_numbering(key, 0)
    number_one = level_numbering(key, 1)
    number_two = level_numbering(key, 2)
    span_x, span_y, span_z, groups = level_shape(0)
    distance = jax.random.randint(jax.random.fold_in(key, 200), (7, groups, N_SLAB, span_x, span_y, span_z), 1, 3).astype(jnp.int32)
    unit = [1] * 7
    tables = {}
    tables['columns'] = spread(by_index(level_links(number_zero, 0, distance), number_zero), 0)
    tables['slots'] = spread(by_index(level_slots(0, distance), number_zero), 0)
    tables['aggregates'] = spread(by_index(level_aggregates(0, number_one), number_zero), 0)
    tables['sends'] = spread(level_sends(number_zero, 0), 0)
    tables['columns_one'] = spread(by_index(level_links(number_one, 1, unit), number_one), 1)
    tables['slots_one'] = spread(by_index(level_slots(1, unit), number_one), 1)
    tables['aggregates_one'] = spread(by_index(level_aggregates(1, number_two), number_one), 1)
    tables['sends_one'] = spread(level_sends(number_one, 1), 1)
    tables['columns_two'] = spread(by_index(level_links(number_two, 2, unit), number_two), 2)
    tables['sends_two'] = spread(level_sends(number_two, 2), 2)
    return tables


def draw_columns(key, part):
    return hierarchy(key)['columns']


def draw_slots(key, part):
    return hierarchy(key)['slots']


def draw_aggregates(key, part):
    return hierarchy(key)['aggregates']


def draw_sends(key, part):
    return hierarchy(key)['sends']


def draw_columns_one(key, part):
    return hierarchy(key)['columns_one']


def draw_slots_one(key, part):
    return hierarchy(key)['slots_one']


def draw_aggregates_one(key, part):
    return hierarchy(key)['aggregates_one']


def draw_sends_one(key, part):
    return hierarchy(key)['sends_one']


def draw_columns_two(key, part):
    return hierarchy(key)['columns_two']


def draw_sends_two(key, part):
    return hierarchy(key)['sends_two']


def draw_prolong_one(key, part):
    span_x, span_y, span_z, groups = level_shape(1)
    shape = (4, 4, groups, N_SLAB, span_x * span_y * span_z)
    subkey = jax.random.fold_in(key, 300)
    values = 0.35 * jnp.clip(jax.random.normal(subkey, shape, jnp.float32), -5.0, 5.0)
    return spread(values, 1)


def draw_operator(key, part):
    count = GX * GY * GZ * N_SUB * N_SLAB
    subkeys = jax.random.split(jax.random.fold_in(key, 400), 4)
    noise = jnp.clip(jax.random.normal(subkeys[0], (7, 4, 4, count), jnp.float32), -4.0, 4.0)
    scale = jnp.ones((1, 4, 1, count), jnp.float32)
    identity = jnp.eye(4, dtype=jnp.float32).reshape(1, 4, 4, 1)
    centre = jnp.exp(jax.random.uniform(subkeys[1], (1, 4, 1, count), jnp.float32, 1.79, 2.64))
    couple = jax.random.uniform(subkeys[2], (6, 4, 1, count), jnp.float32, 0.4, 1.6)
    first = centre * identity + 0.6 * noise[:1] * (1.0 - identity)
    rest = -couple * identity + 0.35 * noise[1:]
    return scale * jnp.concatenate([first, rest], axis=0)


def steps_of(key, shape, shards, least, largest):
    def one(axis_at, blocks):
        draws = jax.random.uniform(jax.random.fold_in(jax.random.fold_in(key, 6), axis_at), (blocks,), jnp.float32, least / len(shards), largest / len(shards))
        return jnp.repeat(jnp.exp(draws), shape[axis_at] // blocks).reshape((-1,) + (1,) * (len(shape) - axis_at - 1))

    gain = one(*shards[0])
    for cut in shards[1:]:
        gain = gain * one(*cut)
    return gain


def centred(rng, extent, width, reach, pieces=(), held_as=jnp.bfloat16):
    drawn = jax.random.normal(rng, extent, jnp.float32) * width
    if len(pieces) > 0:
        drawn = steps_of(rng, extent, pieces, -0.22, 0.18) * drawn
    return jnp.clip(drawn, min=-reach, max=reach).astype(held_as)


def setup_inputs(seed: int = 0) -> dict:
    seeds = jax.random.split(jax.random.key(seed), 15)
    return {
        "source": centred(seeds[0], (4, CELLS * DEVICES), 1.0, 6.0, ((1, 512),), jnp.float32),
        "operator": draw_operator(jax.random.fold_in(seeds[14], 71), 0),
        "prolong": centred(seeds[2], (4, 4, CELLS * DEVICES), 0.35, 2.0, ((2, 512),), jnp.float32),
        "columns": draw_columns(jax.random.fold_in(seeds[14], 71), 0),
        "slots": draw_slots(jax.random.fold_in(seeds[14], 71), 0),
        "aggregates": draw_aggregates(jax.random.fold_in(seeds[14], 71), 0),
        "sends": draw_sends(jax.random.fold_in(seeds[14], 71), 0),
        "prolong_one": draw_prolong_one(jax.random.fold_in(seeds[14], 71), 0),
        "columns_one": draw_columns_one(jax.random.fold_in(seeds[14], 71), 0),
        "slots_one": draw_slots_one(jax.random.fold_in(seeds[14], 71), 0),
        "aggregates_one": draw_aggregates_one(jax.random.fold_in(seeds[14], 71), 0),
        "sends_one": draw_sends_one(jax.random.fold_in(seeds[14], 71), 0),
        "columns_two": draw_columns_two(jax.random.fold_in(seeds[14], 71), 0),
        "sends_two": draw_sends_two(jax.random.fold_in(seeds[14], 71), 0),
    }


def apply_rows(operator, columns, extended):
    nearby = extended[:, columns]
    total = jnp.zeros_like(operator[0, :, 0, :])
    for comp in range(4):
        total = total + jnp.sum(operator[:, :, comp, :] * nearby[comp][:, None, :], axis=0)
    return total


def row_weights(operator):
    return 1.0 + jnp.sum(jnp.abs(operator), axis=(0, 2))


def restrict_rows(prolong, residual, aggregates, coarse):
    lifted = jnp.sum(prolong * residual[:, None, :], axis=0)
    return jnp.zeros((4, coarse), lifted.dtype).at[:, aggregates].add(lifted)


def galerkin_rows(operator, prolong, columns, slots, aggregates, extended, coarse):
    nearby = extended[:, :, columns]
    inner = jnp.zeros((4,) + nearby.shape[1:], nearby.dtype)
    for comp in range(4):
        inner = inner + jnp.transpose(operator[:, :, comp, :], (1, 0, 2))[:, None, :, :] * nearby[comp][None]
    blocks = jnp.zeros_like(inner)
    for comp in range(4):
        blocks = blocks + prolong[comp][:, None, None, :] * inner[comp][None]
    target = (slots * coarse + aggregates[None, :]).reshape(-1)
    total = jnp.zeros((16, 7 * coarse), blocks.dtype).at[:, target].add(blocks.reshape(16, -1))
    return total.reshape(4, 4, 7, coarse).transpose(2, 0, 1, 3)


def to_devices(array):
    lead = array.shape[:-1]
    shaped = array.reshape(lead + (N_SUB, N_SLAB, -1))
    return jnp.moveaxis(shaped, (len(lead), len(lead) + 1), (0, 1))


def from_devices(array):
    moved = jnp.moveaxis(array, (0, 1), (-3, -2))
    return moved.reshape(moved.shape[:-3] + (-1,))


def shift_devices(array, axis, offset):
    rolled = jnp.roll(array, offset, axis=axis)
    count = array.shape[axis]
    anchor = jnp.arange(count) - offset
    valid = (anchor >= 0) & (anchor < count)
    shape = [1] * array.ndim
    shape[axis] = count
    return jnp.where(valid.reshape(shape), rolled, jnp.zeros_like(rolled))


def per_device(function):
    return jax.vmap(jax.vmap(function))


def take_rows(values, sends):
    return values[:, sends]


def extend_all(values, sends, faces, group):
    first_count, second_count = faces
    picked = per_device(take_rows)(values, sends)
    low_first = picked[..., :first_count]
    high_first = picked[..., first_count:2 * first_count]
    low_second = picked[..., 2 * first_count:2 * first_count + second_count]
    high_second = picked[..., 2 * first_count + second_count:]
    parts = [values, shift_devices(high_first, 1, 1), shift_devices(low_first, 1, -1),
             shift_devices(high_second, 0, group), shift_devices(low_second, 0, -group)]
    return jnp.concatenate(parts, axis=-1)


def smooth_all(operator, columns, source, sends, faces, group, final):
    weights = per_device(row_weights)(operator)
    first = source / weights
    residual = source - per_device(apply_rows)(operator, columns, extend_all(first, sends, faces, group))
    second = first + residual / weights
    if final:
        residual = source - per_device(apply_rows)(operator, columns, extend_all(second, sends, faces, group))
    return second, residual


def flatten_lead(array):
    return array.reshape((-1,) + array.shape[2:])


def galerkin_all(operator, prolong, columns, slots, aggregates, sends, faces, group, coarse):
    lead = operator.shape[:2]
    flat_prolong = prolong.reshape(lead + (16, -1))
    extended = extend_all(flat_prolong, sends, faces, group)
    extended = extended.reshape(lead + (4, 4, -1))

    def single(items):
        return galerkin_rows(items[0], items[1], items[2], items[3], items[4], items[5], coarse)

    items = tuple(flatten_lead(item) for item in (operator, prolong, columns, slots, aggregates, extended))
    result = lax.map(single, items)
    return result.reshape(lead + result.shape[1:])


def merge_devices(array, bit):
    count = array.shape[0]
    stride = 1 << bit
    shaped = array.reshape((count // (2 * stride), 2, stride) + array.shape[1:])
    joined = jnp.concatenate([shaped[:, 0], shaped[:, 1]], axis=-1)
    spread = jnp.broadcast_to(joined[:, None], (joined.shape[0], 2) + joined.shape[1:])
    return spread.reshape((count,) + joined.shape[2:])


def own_share(array, members):
    count = array.shape[0]
    shaped = array.reshape((count // members, members) + array.shape[1:-1] + (members, -1))
    picked = [shaped[:, member, ..., member, :] for member in range(members)]
    stacked = jnp.stack(picked, axis=1)
    return stacked.reshape((count,) + stacked.shape[2:])


def reference(source, operator, prolong, columns, slots, aggregates, sends, prolong_one, columns_one, slots_one, aggregates_one, sends_one, columns_two, sends_two):
    faces_zero = (2 * GY * GZ, 2 * GX * GZ)
    faces_one = (GY * (GZ // 2), (GX // 2) * (GZ // 2))
    faces_two = (GY * (GZ // 4), (GX // 4) * (GZ // 4))
    rows_one = GX * GY * GZ // 8
    coarse_two = rows_one // 4
    source_dev = to_devices(source)
    operator_dev = to_devices(operator)
    prolong_dev = to_devices(prolong)
    columns_dev = to_devices(columns)
    slots_dev = to_devices(slots)
    aggregates_dev = to_devices(aggregates)
    sends_dev = to_devices(sends)
    prolong_one_dev = to_devices(prolong_one)
    columns_one_dev = to_devices(columns_one)
    slots_one_dev = to_devices(slots_one)
    aggregates_one_dev = to_devices(aggregates_one)
    sends_one_dev = to_devices(sends_one)
    columns_two_dev = to_devices(columns_two)
    sends_two_dev = to_devices(sends_two)

    smoothed, residual = smooth_all(operator_dev, columns_dev, source_dev, sends_dev, faces_zero, 1, True)
    source_own = per_device(partial(restrict_rows, coarse=rows_one))(prolong_dev, residual, aggregates_dev)
    operator_own = galerkin_all(operator_dev, prolong_dev, columns_dev, slots_dev, aggregates_dev, sends_dev, faces_zero, 1, rows_one)
    source_merged = merge_devices(source_own, 0)
    operator_merged = merge_devices(operator_own, 0)
    smooth_one, residual_one = smooth_all(operator_merged, columns_one_dev, source_merged, sends_one_dev, faces_one, 2, True)
    source_pair = per_device(partial(restrict_rows, coarse=coarse_two))(prolong_one_dev, residual_one, aggregates_one_dev)
    operator_pair = galerkin_all(operator_merged, prolong_one_dev, columns_one_dev, slots_one_dev, aggregates_one_dev, sends_one_dev, faces_one, 2, coarse_two)
    source_group = merge_devices(source_pair, 1)
    operator_group = merge_devices(operator_pair, 1)
    smooth_two, unused = smooth_all(operator_group, columns_two_dev, source_group, sends_two_dev, faces_two, 4, False)
    return from_devices(smoothed), from_devices(own_share(smooth_one, 2)), from_devices(own_share(smooth_two, 4))
```

```python
import jax
import jax.numpy as jnp
from jax import lax
from jax.experimental import pallas as pl
from jax.experimental.pallas import tpu as pltpu
from jax.sharding import PartitionSpec as P

F32 = jnp.float32
BF16 = jnp.bfloat16
MESH = pl.DeviceIdType.MESH

FIRST0, SECOND0, PROLONG0, PROLONG1, FIRST1, SECOND1, FIRST2, OP1, SRC1, OP2, SRC2 = range(11)


def loop(count, body, init=0):
    return lax.fori_loop(0, count, body, init, unroll=True)


def lookup(index, init, base, count, row, flip=0):
    lane = (index & 127) ^ flip if flip else index & 127
    high = index >> 7
    channels = len(init)

    def body(j, held):
        here = high == base + j
        out = []
        for c in range(channels):
            spread = jnp.broadcast_to(row(c, j), index.shape)
            out.append(jnp.where(here, jnp.take_along_axis(spread, lane, axis=1), held[c]))
        return tuple(out)

    return loop(count, body, tuple(init))


def split(value):
    high = value.astype(BF16)
    return high, (value - high.astype(F32)).astype(BF16)


def against(left, right):
    return lax.dot_general(left, right, (((1,), (1,)), ((), ())), preferred_element_type=F32)


def kernel(
    source_ref, operator_ref, prolong_ref, columns_ref, slots_ref, aggregates_ref, sends_ref,
    prolong_one_ref, columns_one_ref, slots_one_ref, aggregates_one_ref, sends_one_ref,
    columns_two_ref, sends_two_ref,
    smoothed_ref, smoothed_one_ref, smoothed_two_ref,
    turn, index0, slot0, op0, src0, weight0, table0, prolong0, near0, nearp0, blocks0, parts0,
    left0, member0, lifted0, lifted0w, pick_a, pick_b, pick_p, ghost_a, ghost_b, ghost_p,
    op1, src1, index1, slot1, prolong1, table1, near1, nearp1, blocks1, parts1, left1, member1,
    lifted1, lifted1w, x1, send1, pick1_p, pick1_a, pick1_b, ghost1_p, ghost1_a, ghost1_b,
    op2, op2x, src2, src2x, pick2, ghost2, send_sem, recv_sem,
):
    sub = lax.axis_index("sub")
    slab = lax.axis_index("slab")
    n_sub = lax.axis_size("sub")
    n_slab = lax.axis_size("slab")
    parity = lax.rem(sub, 2)
    quad = lax.rem(sub // 2, 2)
    has_before = slab > 0
    has_after = slab < n_slab - 1

    barrier = pltpu.get_barrier_semaphore()
    greeted = [(has_before, (sub, slab - 1)), (has_after, (sub, slab + 1))]
    for far in (1, 2, 4):
        greeted += [(sub >= far, (sub - far, slab)), (sub < n_sub - far, (sub + far, slab))]
    for there, peer in greeted:
        @pl.when(there)
        def _(peer=peer):
            pl.semaphore_signal(barrier, inc=1, device_id=peer, device_id_type=MESH)

    def routes(far):
        after = (has_after, (sub, slab + 1))
        before = (has_before, (sub, slab - 1))
        upper = (sub < n_sub - far, (sub + far, slab))
        lower = (sub >= far, (sub - far, slab))
        return [(after, before), (before, after), (upper, lower), (lower, upper)]

    def copy(name, d, piece, ghost, peer):
        return pltpu.make_async_remote_copy(
            piece, ghost, send_sem.at[name, d], recv_sem.at[name, d], device_id=peer, device_id_type=MESH
        )

    def send(name, far, pieces, ghost):
        for d, (to, _) in enumerate(routes(far)):
            @pl.when(to[0])
            def _(d=d, to=to):
                copy(name, d, pieces[d], ghost.at[d], to[1]).start()

    def receive(name, far, pieces, ghost):
        for d, (_, source) in enumerate(routes(far)):
            @pl.when(source[0])
            def _(d=d, source=source):
                copy(name, d, pieces[d], ghost.at[d], source[1]).wait_recv()

    def finish(name, far, pieces, ghost):
        for d, (to, _) in enumerate(routes(far)):
            @pl.when(to[0])
            def _(d=d, to=to):
                copy(name, d, pieces[d], ghost.at[d], to[1]).wait_send()

    def clear(far, ghosts):
        for d, (_, source) in enumerate(routes(far)):
            @pl.when(jnp.logical_not(source[0]))
            def _(d=d):
                for ghost in ghosts:
                    ghost[d] = jnp.zeros_like(ghost[d])

    clear(1, (ghost_a, ghost_b, ghost_p))
    clear(2, (ghost1_a, ghost1_b, ghost1_p))
    clear(4, (ghost2,))

    for h in range(2):
        for a in range(4):
            src0[a, h] = source_ref[pl.ds(32 * h + a, 8, 4), :]

    def weigh(a, _):
        for h in range(2):
            def slot_body(k, total):
                for c in range(4):
                    value = operator_ref[4 * k + a, pl.ds(32 * h + c, 8, 4), :]
                    op0[16 * k + 4 * a + c, h] = value
                    total = total + jnp.abs(value)
                return total

            total = loop(7, slot_body, jnp.ones((8, 128), F32))
            weight0[a, h] = total
            table0[a, h] = src0[a, h] / total
        return 0

    lax.fori_loop(0, 4, weigh, 0)

    zeros = tuple(jnp.zeros((8, 128), F32) for _ in range(4))

    def pick0(table, pick, group):
        def one(h, _):
            index = sends_ref[pl.ds(pl.multiple_of(8 * h, 8), 8), :]
            got = lookup(index, zeros, 0, 16, lambda c, j: table[4 * group + c, j // 8, pl.ds(j % 8, 1), :])
            for c in range(4):
                pick[2 * h, 4 * group + c] = got[c][0:4]
                pick[2 * h + 1, 4 * group + c] = got[c][4:8]
            return 0

        lax.fori_loop(0, 2, one, 0)

    def faces0(pick):
        return [pick.at[1], pick.at[0], pick.at[3], pick.at[2]]

    pick0(table0, pick_a, 0)

    present = sum(there.astype(jnp.int32) for there, _ in greeted)
    pl.semaphore_wait(barrier, present)

    send(FIRST0, 1, faces0(pick_a), ghost_a)

    def spread_prolong(a, _):
        for h in range(2):
            for b in range(4):
                prolong0[4 * a + b, h] = prolong_ref[a, pl.ds(32 * h + b, 8, 4), :]
        return 0

    lax.fori_loop(0, 4, spread_prolong, 0)

    def pick_prolong(group, _):
        pick0(prolong0, pick_p, group)
        return 0

    lax.fori_loop(0, 4, pick_prolong, 0)
    send(PROLONG0, 1, faces0(pick_p), ghost_p)

    for g in range(4):
        for a in range(4):
            prolong1[pl.ds(16 * a + g, 4, 4), :] = prolong_one_ref[a, :, pl.ds(128 * g, 128)]
        index1[pl.ds(g, 7, 4), :] = columns_one_ref[:, pl.ds(128 * g, 128)]
        slot1[pl.ds(g, 7, 4), :] = slots_one_ref[:, pl.ds(128 * g, 128)]
    index1[28:32] = jnp.zeros((4, 128), jnp.int32)
    send1[...] = jnp.zeros((8, 128), jnp.int32)
    send1[0:3] = sends_one_ref[...]

    def pick1(table, pick, group):
        index = send1[...]
        got = lookup(index, zeros, 0, 4, lambda c, j: table[pl.ds(4 * (4 * group + c) + j, 1), :])
        for c in range(4):
            for r in range(3):
                pick[r, pl.ds(4 * group + c, 1), :] = got[c][r:r + 1]

    def faces1(pick):
        return [pick.at[1], pick.at[0], pick.at[2], pick.at[2]]

    for group in range(4):
        pick1(prolong1, pick1_p, group)
    send(PROLONG1, 2, faces1(pick1_p), ghost1_p)

    for j in range(16):
        turn[8 * j:8 * j + 7] = columns_ref[:, pl.ds(128 * j, 128)]
    for k in range(7):
        for h in range(2):
            index0[2 * k + h] = turn[pl.ds(64 * h + k, 8, 8), :]
    for j in range(16):
        turn[8 * j:8 * j + 7] = slots_ref[:, pl.ds(128 * j, 128)]
    for k in range(7):
        for h in range(2):
            slot0[2 * k + h] = turn[pl.ds(64 * h + k, 8, 8), :]

    def own0(table, near, v, group):
        got = lookup(index0[v], zeros, 0, 16, lambda c, j: table[4 * group + c, j // 8, pl.ds(j % 8, 1), :])
        for c in range(4):
            near[4 * group + c, v] = got[c]

    def ghost0(ghost, near, v, group):
        held = tuple(near[4 * group + c, v] for c in range(4))
        got = lookup(index0[v], held, 16, 16, lambda c, j: ghost[j // 4, 4 * group + c, pl.ds(j % 4, 1), :])
        for c in range(4):
            near[4 * group + c, v] = got[c]

    def residual0(h):
        totals = []
        for a in range(4):
            def body(k, total):
                for c in range(4):
                    total = total + op0[16 * k + 4 * a + c, h] * near0[c, 2 * k + h]
                return total

            totals.append(src0[a, h] - loop(7, body, jnp.zeros((8, 128), F32)))
        return totals

    def each(count, function):
        def body(i, _):
            function(i)
            return 0

        lax.fori_loop(0, count, body, 0)

    each(14, lambda v: own0(table0, near0, v, 0))
    each(56, lambda i: own0(prolong0, nearp0, i // 4, i % 4))
    receive(FIRST0, 1, faces0(pick_a), ghost_a)
    each(14, lambda v: ghost0(ghost_a, near0, v, 0))
    for h in range(2):
        rest = residual0(h)
        for a in range(4):
            value = table0[a, h] + rest[a] / weight0[a, h]
            table0[a, h] = value
            smoothed_ref[pl.ds(32 * h + a, 8, 4), :] = value
    pick0(table0, pick_b, 0)
    send(SECOND0, 1, faces0(pick_b), ghost_b)

    each(14, lambda v: own0(table0, near0, v, 0))
    for j in range(16):
        rows = lax.broadcasted_iota(jnp.int32, (256, 128), 0)
        member0[:, pl.ds(128 * j, 128)] = jnp.where(
            rows == aggregates_ref[j:j + 1, :], 1.0, 0.0
        ).astype(BF16)
    receive(PROLONG0, 1, faces0(pick_p), ghost_p)
    each(56, lambda i: ghost0(ghost_p, nearp0, i // 4, i % 4))

    def product0(v):
        k, h = v // 2, v % 2
        for d in range(4):
            near = [nearp0[4 * c + d, v] for c in range(4)]
            inner = []
            for a in range(4):
                total = op0[16 * k + 4 * a, h] * near[0]
                for c in range(1, 4):
                    total = total + op0[16 * k + 4 * a + c, h] * near[c]
                inner.append(total)
            for b in range(4):
                total = prolong0[b, h] * inner[0]
                for a in range(1, 4):
                    total = total + prolong0[4 * a + b, h] * inner[a]
                blocks0[v, 4 * b + d] = total

    each(14, product0)

    def gather_slots0(i):
        bd, h = i // 2, i % 2
        blocks = [blocks0[2 * k + h, bd] for k in range(7)]
        slots = [slot0[2 * k + h] for k in range(7)]
        for s in range(7):
            total = jnp.zeros((8, 128), F32)
            for k in range(7):
                total = total + jnp.where(slots[k] == s, blocks[k], 0.0)
            parts0[pl.ds(pl.multiple_of(256 * s + 16 * bd + 8 * h, 8), 8), :] = total

    each(32, gather_slots0)
    for j in range(16):
        high, low = split(parts0[pl.ds(j, 112, 16), :])
        left0[0:112, pl.ds(128 * j, 128)] = high
        left0[112:224, pl.ds(128 * j, 128)] = low
    both = against(left0[...], member0[...])
    coarse = both[0:112] + both[112:224]
    half = pl.multiple_of(224 * parity, 8)
    for jj in range(2):
        op1[pl.ds(half + 112 * jj, 112), :] = coarse[:, 128 * jj:128 * jj + 128]

    partner = (sub + 1 - 2 * parity, slab)
    mate = (sub + 2 - 4 * quad, slab)
    op1_half = op1.at[pl.ds(half, 224), :]
    op1_other = op1.at[pl.ds(pl.multiple_of(224 - 224 * parity, 8), 224), :]
    copy(OP1, 0, op1_half, op1_half, partner).start()

    receive(SECOND0, 1, faces0(pick_b), ghost_b)
    each(14, lambda v: ghost0(ghost_b, near0, v, 0))
    for h in range(2):
        rest = residual0(h)
        for b in range(4):
            total = prolong0[b, h] * rest[0]
            for a in range(1, 4):
                total = total + prolong0[4 * a + b, h] * rest[a]
            lifted0[pl.ds(32 * h + b, 8, 4), :] = total
    for j in range(16):
        value = lifted0[4 * j:4 * j + 4]
        lifted0w[0:4, pl.ds(128 * j, 128)] = value
        lifted0w[4:8, pl.ds(128 * j, 128)] = value - value.astype(BF16).astype(F32)
    both = against(lifted0w[...].astype(BF16), member0[...])
    coarse = both[0:4] + both[4:8]
    for jj in range(2):
        src1[2 * parity + jj] = coarse[:, 128 * jj:128 * jj + 128]
    src1_half = src1.at[pl.ds(2 * parity, 2)]
    src1_other = src1.at[pl.ds(2 - 2 * parity, 2)]
    copy(SRC1, 0, src1_half, src1_half, partner).start()

    def own1(table, near, v, group):
        index = index1[pl.ds(pl.multiple_of(8 * v, 8), 8), :]
        got = lookup(index, zeros, 0, 4, lambda c, j: table[pl.ds(4 * (4 * group + c) + j, 1), :])
        for c in range(4):
            near[4 * group + c, pl.ds(pl.multiple_of(8 * v, 8), 8), :] = got[c]

    upper_lanes = lax.broadcasted_iota(jnp.int32, (1, 128), 1) >= 64

    def ghost1(ghost, near, v, group):
        rows = pl.ds(pl.multiple_of(8 * v, 8), 8)
        index = index1[rows, :]
        got = tuple(near[4 * group + c, rows, :] for c in range(4))
        got = lookup(index, got, 4, 2, lambda c, j: ghost[j, pl.ds(4 * group + c, 1), :])

        def last(c, j):
            channel = pl.ds(4 * group + c, 1)
            return jnp.where(upper_lanes, ghost[2, channel, :], ghost[3, channel, :])

        got = lookup(index, got, 6, 1, last, flip=64)
        for c in range(4):
            near[4 * group + c, rows, :] = got[c]

    each(16, lambda i: own1(prolong1, nearp1, i // 4, i % 4))
    receive(PROLONG1, 2, faces1(pick1_p), ghost1_p)
    each(16, lambda i: ghost1(ghost1_p, nearp1, i // 4, i % 4))
    for g in range(4):
        rows = lax.broadcasted_iota(jnp.int32, (128, 128), 0)
        member1[:, pl.ds(128 * g, 128)] = jnp.where(
            rows == aggregates_one_ref[g:g + 1, :] + 64 * quad, 1.0, 0.0
        ).astype(BF16)

    copy(OP1, 0, op1_half, op1_other, partner).wait_recv()

    def block1(k, a, c):
        return op1[pl.ds(16 * k + 4 * a + c, 4, 112), :]

    weight1 = []
    for a in range(4):
        def body(k, total):
            for c in range(4):
                total = total + jnp.abs(block1(k, a, c))
            return total

        weight1.append(loop(7, body, jnp.ones((4, 128), F32)))

    copy(SRC1, 0, src1_half, src1_other, partner).wait_recv()

    source1 = []
    first1 = []
    for a in range(4):
        source1.append(jnp.concatenate([src1[g, a:a + 1, :] for g in range(4)], axis=0))
        first1.append(source1[a] / weight1[a])
        table1[4 * a:4 * a + 4] = first1[a]
    pick1(table1, pick1_a, 0)
    send(FIRST1, 2, faces1(pick1_a), ghost1_a)
    each(4, lambda v: own1(table1, near1, v, 0))

    def product1(k):
        for d in range(4):
            near = [nearp1[4 * c + d, pl.ds(4 * k, 4), :] for c in range(4)]
            inner = []
            for a in range(4):
                total = block1(k, a, 0) * near[0]
                for c in range(1, 4):
                    total = total + block1(k, a, c) * near[c]
                inner.append(total)
            for b in range(4):
                total = prolong1[4 * b:4 * b + 4] * inner[0]
                for a in range(1, 4):
                    total = total + prolong1[16 * a + 4 * b:16 * a + 4 * b + 4] * inner[a]
                blocks1[k, 4 * b + d] = total

    each(7, product1)

    def gather_slots1(bd):
        blocks = [blocks1[k, bd] for k in range(7)]
        slots = [slot1[4 * k:4 * k + 4] for k in range(7)]
        for s in range(7):
            total = jnp.zeros((4, 128), F32)
            for k in range(7):
                total = total + jnp.where(slots[k] == s, blocks[k], 0.0)
            parts1[16 * s + bd] = total

    each(16, gather_slots1)
    for g in range(4):
        high, low = split(parts1[:, g, :])
        left1[0:112, pl.ds(128 * g, 128)] = high
        left1[112:224, pl.ds(128 * g, 128)] = low
    both = against(left1[...], member1[...])
    op2[...] = both[0:112] + both[112:224]
    copy(OP2, 0, op2, op2x, mate).start()

    def residual1():
        totals = []
        for a in range(4):
            def body(k, total):
                for c in range(4):
                    total = total + block1(k, a, c) * near1[c, pl.ds(4 * k, 4), :]
                return total

            totals.append(source1[a] - loop(7, body, jnp.zeros((4, 128), F32)))
        return totals

    receive(FIRST1, 2, faces1(pick1_a), ghost1_a)
    each(4, lambda v: ghost1(ghost1_a, near1, v, 0))
    rest = residual1()
    for a in range(4):
        value = first1[a] + rest[a] / weight1[a]
        table1[4 * a:4 * a + 4] = value
        x1[pl.ds(a, 4, 4), :] = value
    pick1(table1, pick1_b, 0)
    send(SECOND1, 2, faces1(pick1_b), ghost1_b)
    each(4, lambda v: own1(table1, near1, v, 0))
    for jj in range(2):
        smoothed_one_ref[:, 128 * jj:128 * jj + 128] = jnp.where(
            parity == 0, x1[4 * jj:4 * jj + 4], x1[8 + 4 * jj:12 + 4 * jj]
        )
    copy(OP2, 0, op2, op2x, mate).wait_recv()
    copy(OP2, 0, op2, op2x, mate).wait_send()
    op2[...] = op2[...] + op2x[...]
    block2 = [[op2[pl.ds(4 * a + c, 7, 16), :] for c in range(4)] for a in range(4)]
    weight2 = []
    for a in range(4):
        total = jnp.abs(block2[a][0])
        for c in range(1, 4):
            total = total + jnp.abs(block2[a][c])
        weight2.append(1.0 + jnp.sum(total, axis=0, keepdims=True))

    receive(SECOND1, 2, faces1(pick1_b), ghost1_b)
    each(4, lambda v: ghost1(ghost1_b, near1, v, 0))
    rest = residual1()
    for b in range(4):
        total = prolong1[4 * b:4 * b + 4] * rest[0]
        for a in range(1, 4):
            total = total + prolong1[16 * a + 4 * b:16 * a + 4 * b + 4] * rest[a]
        lifted1[pl.ds(b, 4, 4), :] = total
    for g in range(4):
        value = lifted1[4 * g:4 * g + 4]
        lifted1w[0:4, pl.ds(128 * g, 128)] = value
        lifted1w[4:8, pl.ds(128 * g, 128)] = value - value.astype(BF16).astype(F32)
    both = against(lifted1w[...].astype(BF16), member1[...])
    src2[...] = both[0:4] + both[4:8]
    copy(SRC2, 0, src2, src2x, mate).start()

    index = columns_two_ref[...]
    lane = lax.broadcasted_iota(jnp.int32, (1, 128), 1)
    copy(SRC2, 0, src2, src2x, mate).wait_recv()
    source2 = src2[...] + src2x[...]
    first2 = [source2[a:a + 1] / weight2[a] for a in range(4)]
    wide = tuple(jnp.zeros((7, 128), F32) for _ in range(4))
    picks = lookup(
        jnp.broadcast_to(sends_two_ref[0:1, :], (8, 128)), zeros, 0, 1, lambda c, j: first2[c]
    )
    for c in range(4):
        pick2[0, c:c + 1] = picks[c][0:1]
    picks = lookup(
        jnp.broadcast_to(sends_two_ref[1:2, :], (8, 128)), zeros, 0, 1, lambda c, j: first2[c]
    )
    for c in range(4):
        pick2[1, c:c + 1] = picks[c][0:1]
    faces2 = [pick2.at[0], pick2.at[0], pick2.at[1], pick2.at[1]]
    send(FIRST2, 4, faces2, ghost2)
    near = lookup(index, wide, 0, 1, lambda c, j: first2[c])
    receive(FIRST2, 4, faces2, ghost2)
    near = lookup(
        index, near, 1, 1, lambda c, j: jnp.where(lane >= 64, ghost2[0, c:c + 1], ghost2[1, c:c + 1]), flip=64
    )
    near = lookup(
        index, near, 2, 1, lambda c, j: jnp.where(lane >= 16, ghost2[2, c:c + 1], ghost2[3, c:c + 1]), flip=16
    )
    place = lax.rem(sub, 4)
    for a in range(4):
        total = block2[a][0] * near[0]
        for c in range(1, 4):
            total = total + block2[a][c] * near[c]
        rest2 = source2[a:a + 1] - jnp.sum(total, axis=0, keepdims=True)
        value = first2[a] + rest2 / weight2[a]
        share = value[:, 0:32]
        for q in range(1, 4):
            share = jnp.where(place == q, value[:, 32 * q:32 * q + 32], share)
        smoothed_two_ref[a:a + 1, :] = share

    finish(FIRST0, 1, faces0(pick_a), ghost_a)
    finish(PROLONG0, 1, faces0(pick_p), ghost_p)
    finish(PROLONG1, 2, faces1(pick1_p), ghost1_p)
    finish(SECOND0, 1, faces0(pick_b), ghost_b)
    finish(FIRST1, 2, faces1(pick1_a), ghost1_a)
    finish(SECOND1, 2, faces1(pick1_b), ghost1_b)
    finish(FIRST2, 4, faces2, ghost2)
    copy(OP1, 0, op1_half, op1_half, partner).wait_send()
    copy(SRC1, 0, src1_half, src1_half, partner).wait_send()
    copy(SRC2, 0, src2, src2x, mate).wait_send()


def fold(array):
    lead = array.shape[:-2]
    shaped = array.reshape(lead + (array.shape[-2], 16, 128))
    return jnp.swapaxes(shaped, -3, -2).reshape(lead + (16 * array.shape[-2], 128))


def on_device(
    source, operator, prolong, columns, slots, aggregates, sends,
    prolong_one, columns_one, slots_one, aggregates_one, sends_one, columns_two, sends_two,
):
    vmem = pl.BlockSpec(memory_space=pltpu.VMEM)
    scratch = [
        ((128, 128), jnp.int32), ((14, 8, 128), jnp.int32), ((14, 8, 128), jnp.int32),
        ((112, 2, 8, 128), F32), ((4, 2, 8, 128), F32), ((4, 2, 8, 128), F32), ((4, 2, 8, 128), F32),
        ((16, 2, 8, 128), F32), ((4, 14, 8, 128), F32), ((16, 14, 8, 128), F32),
        ((14, 16, 8, 128), F32), ((1792, 128), F32), ((224, 2048), BF16), ((256, 2048), BF16),
        ((64, 128), F32), ((8, 2048), F32),
        ((4, 4, 4, 128), F32), ((4, 4, 4, 128), F32), ((4, 16, 4, 128), F32),
        ((4, 4, 4, 128), F32), ((4, 4, 4, 128), F32), ((4, 16, 4, 128), F32),
        ((448, 128), F32), ((4, 4, 128), F32), ((32, 128), jnp.int32), ((32, 128), jnp.int32),
        ((64, 128), F32), ((16, 128), F32), ((4, 32, 128), F32), ((16, 32, 128), F32),
        ((7, 16, 4, 128), F32), ((112, 4, 128), F32), ((224, 512), BF16), ((128, 512), BF16),
        ((16, 128), F32), ((8, 512), F32), ((16, 128), F32), ((8, 128), jnp.int32),
        ((3, 16, 128), F32), ((3, 4, 128), F32), ((3, 4, 128), F32),
        ((4, 16, 128), F32), ((4, 4, 128), F32), ((4, 4, 128), F32),
        ((112, 128), F32), ((112, 128), F32), ((4, 128), F32), ((4, 128), F32),
        ((2, 4, 128), F32), ((4, 4, 128), F32),
    ]
    smoothed, smoothed_one, smoothed_two = pl.pallas_call(
        kernel,
        out_shape=(
            jax.ShapeDtypeStruct((64, 128), F32),
            jax.ShapeDtypeStruct((4, 256), F32),
            jax.ShapeDtypeStruct((4, 32), F32),
        ),
        in_specs=[vmem] * 14,
        out_specs=(vmem,) * 3,
        scratch_shapes=[pltpu.VMEM(shape, kind) for shape, kind in scratch]
        + [pltpu.SemaphoreType.DMA((11, 4)), pltpu.SemaphoreType.DMA((11, 4))],
        compiler_params=pltpu.CompilerParams(
            collective_id=0, has_side_effects=True, vmem_limit_bytes=48 << 20
        ),
        name="descend",
    )(
        fold(source), fold(operator).reshape(28, 64, 128), fold(prolong), columns, slots,
        aggregates.reshape(16, 128), sends.reshape(16, 128),
        prolong_one, columns_one, slots_one, aggregates_one.reshape(4, 128), sends_one.reshape(3, 128),
        columns_two, jnp.pad(sends_two, (0, 96)).reshape(2, 128),
    )
    smoothed = smoothed.reshape(16, 4, 128).swapaxes(0, 1).reshape(4, 2048)
    return smoothed, smoothed_one, smoothed_two


def solution(mesh):
    both = ("sub", "slab")
    flat = P(both)
    rows = P(None, both)
    blocks = P(None, None, both)
    placed = (
        rows, P(None, None, None, both), blocks, rows, rows, flat, flat,
        blocks, rows, rows, flat, flat, rows, flat,
    )
    return jax.shard_map(
        on_device, mesh=mesh, in_specs=placed, out_specs=(rows, rows, rows), check_vma=False
    )
```

```python
import jax
import jax.numpy as jnp
from jax import lax
from jax.experimental import pallas as pl
from jax.experimental.pallas import tpu as pltpu
from jax.sharding import PartitionSpec as P

F32 = jnp.float32
BF16 = jnp.bfloat16
MESH = pl.DeviceIdType.MESH

FIRST0, SECOND0, PROLONG0, PROLONG1, FIRST1, SECOND1, FIRST2, OP1, SRC1, OP2, SRC2 = range(11)


def loop(count, body, init=0):
    return lax.fori_loop(0, count, body, init, unroll=True)


LANES = lax.GatherDimensionNumbers(
    offset_dims=(), collapsed_slice_dims=(1,), start_index_map=(1,),
    operand_batching_dims=(0,), start_indices_batching_dims=(0,),
)


def pick_lanes(values, lanes):
    return lax.gather(
        values, lanes[..., None], LANES, slice_sizes=(1, 1), mode=lax.GatherScatterMode.PROMISE_IN_BOUNDS
    )


def lookup(indices, init, base, count, row, flip=0):
    lanes = [(index & 127) ^ flip if flip else index & 127 for index in indices]
    highs = [index >> 7 for index in indices]
    channels = len(init[0])

    held = [list(tile) for tile in init]
    for j in range(count):
        here = [high == base + j for high in highs]
        for c in range(channels):
            spread = jnp.broadcast_to(row(c, j), indices[0].shape)
            for v, lane in enumerate(lanes):
                held[v][c] = jnp.where(here[v], pick_lanes(spread, lane), held[v][c])
    return held


def split(value):
    high = value.astype(BF16)
    return high, (value - high.astype(F32)).astype(BF16)


def against(left, right):
    return lax.dot_general(left, right, (((1,), (1,)), ((), ())), preferred_element_type=F32)


def kernel(
    source_in, operator_in, prolong_in, columns_in, slots_in, aggregates_in, sends_in,
    prolong_one_in, columns_one_in, slots_one_in, aggregates_one_in, sends_one_in,
    columns_two_in, sends_two_in,
    result_ref,
    source_ref, operator_ref, prolong_ref, columns_ref, slots_ref, aggregates_ref, sends_ref,
    prolong_one_ref, columns_one_ref, slots_one_ref, aggregates_one_ref, sends_one_ref,
    columns_two_ref, sends_two_ref,
    turn, index0, slot0, op0, src0, weight0, table0, prolong0, near0, nearp0, blocks0, parts0,
    left0, member0, lifted0, lifted0w, pick_a, pick_b, pick_p, ghost_a, ghost_b, ghost_p,
    op1, src1, index1, slot1, prolong1, table1, near1, nearp1, blocks1, parts1, left1, member1,
    lifted1, lifted1w, x1, send1, pick1_p, pick1_a, pick1_b, ghost1_p, ghost1_a, ghost1_b,
    op2, op2x, src2, src2x, pick2, ghost2, table_p, terms_p, load_sem, send_sem, recv_sem,
):
    inputs = [
        (sends_in, sends_ref), (prolong_in, prolong_ref), (source_in, source_ref), (operator_in, operator_ref),
        (columns_in, columns_ref), (prolong_one_in, prolong_one_ref), (sends_one_in, sends_one_ref),
        (aggregates_in, aggregates_ref), (slots_in, slots_ref), (columns_one_in, columns_one_ref),
        (slots_one_in, slots_one_ref), (aggregates_one_in, aggregates_one_ref),
        (columns_two_in, columns_two_ref), (sends_two_in, sends_two_ref),
    ]
    loads = {
        id(place): pltpu.make_async_copy(given, place, load_sem.at[i]) for i, (given, place) in enumerate(inputs)
    }
    for _, place in inputs:
        loads[id(place)].start()

    def landed(*places):
        for place in places:
            loads[id(place)].wait()

    sub = lax.axis_index("sub")
    slab = lax.axis_index("slab")
    n_sub = lax.axis_size("sub")
    n_slab = lax.axis_size("slab")
    parity = lax.rem(sub, 2)
    quad = lax.rem(sub // 2, 2)
    has_before = slab > 0
    has_after = slab < n_slab - 1

    barrier = pltpu.get_barrier_semaphore()
    greeted = [(has_before, (sub, slab - 1)), (has_after, (sub, slab + 1))]
    for far in (1, 2, 4):
        greeted += [(sub >= far, (sub - far, slab)), (sub < n_sub - far, (sub + far, slab))]
    for there, peer in greeted:
        @pl.when(there)
        def _(peer=peer):
            pl.semaphore_signal(barrier, inc=1, device_id=peer, device_id_type=MESH)

    def routes(far):
        after = (has_after, (sub, slab + 1))
        before = (has_before, (sub, slab - 1))
        upper = (sub < n_sub - far, (sub + far, slab))
        lower = (sub >= far, (sub - far, slab))
        return [(after, before), (before, after), (upper, lower), (lower, upper)]

    def copy(name, d, piece, ghost, peer):
        return pltpu.make_async_remote_copy(
            piece, ghost, send_sem.at[name, d], recv_sem.at[name, d], device_id=peer, device_id_type=MESH
        )

    def part(ghost, d):
        return ghost[d] if isinstance(ghost, list) else ghost.at[d]

    def send(name, far, pieces, ghost):
        for d, (to, _) in enumerate(routes(far)):
            @pl.when(to[0])
            def _(d=d, to=to):
                copy(name, d, pieces[d], part(ghost, d), to[1]).start()

    def receive(name, far, pieces, ghost):
        for d, (_, source) in enumerate(routes(far)):
            @pl.when(source[0])
            def _(d=d, source=source):
                copy(name, d, pieces[d], part(ghost, d), source[1]).wait_recv()

    def finish(name, far, pieces, ghost):
        for d, (to, _) in enumerate(routes(far)):
            @pl.when(to[0])
            def _(d=d, to=to):
                copy(name, d, pieces[d], part(ghost, d), to[1]).wait_send()

    def clear(far, ghosts):
        for d, (_, source) in enumerate(routes(far)):
            @pl.when(jnp.logical_not(source[0]))
            def _(d=d):
                for ghost in ghosts:
                    ghost[d] = jnp.zeros_like(ghost[d])

    clear(1, (ghost_a, ghost_b))
    for d, (_, giver) in enumerate(routes(1)):
        @pl.when(jnp.logical_not(giver[0]))
        def _(d=d):
            ghost_p[64 * d:64 * d + 64] = jnp.zeros((64, 128), F32)
    clear(2, (ghost1_a, ghost1_b, ghost1_p))
    clear(4, (ghost2,))

    zeros = tuple(jnp.zeros((8, 128), F32) for _ in range(4))

    def pick0(row, group, keep):
        got = lookup([sends_ref[0:8, :], sends_ref[8:16, :]], (zeros,) * 2, 0, 16, lambda c, j: row(4 * group + c, j))
        for h in range(2):
            for c in range(4):
                keep(h, 4 * group + c, got[h][c])

    def keep_in(pick):
        def keep(h, c, got):
            pick[2 * h, c] = got[0:4]
            pick[2 * h + 1, c] = got[4:8]

        return keep

    def keep_prolong(h, c, got):
        pick_p[pl.ds(128 * h + c, 8, 16), :] = got

    def table_row(c, j):
        return table0[c, j // 8, pl.ds(j % 8, 1), :]

    def faces0(pick):
        return [pick.at[1], pick.at[0], pick.at[3], pick.at[2]]

    faces_p = [pick_p.at[pl.ds(64 * d, 64), :] for d in (1, 0, 3, 2)]
    ghosts_p = [ghost_p.at[pl.ds(64 * d, 64), :] for d in range(4)]

    landed(sends_ref, prolong_ref)

    def spread_prolong(a, _):
        for h in range(2):
            for b in range(4):
                prolong0[4 * a + b, h] = prolong_ref[a, pl.ds(32 * h + b, 8, 4), :]
        return 0

    lax.fori_loop(0, 4, spread_prolong, 0, unroll=True)

    def pick_prolong(group, _):
        pick0(lambda c, j: prolong0[c, j // 8, pl.ds(j % 8, 1), :], group, keep_prolong)
        return 0

    lax.fori_loop(0, 4, pick_prolong, 0)

    landed(source_ref, operator_ref)
    for h in range(2):
        for a in range(4):
            src0[a, h] = source_ref[pl.ds(32 * h + a, 8, 4), :]

    def weigh(a, _):
        for h in range(2):
            def slot_body(k, total):
                for c in range(4):
                    value = operator_ref[4 * k + a, pl.ds(32 * h + c, 8, 4), :]
                    op0[16 * k + 4 * a + c, h] = value
                    total = total + jnp.abs(value)
                return total

            total = loop(7, slot_body, jnp.ones((8, 128), F32))
            weight0[a, h] = total
            table0[a, h] = src0[a, h] / total
        return 0

    lax.fori_loop(0, 4, weigh, 0)
    pick0(table_row, 0, keep_in(pick_a))

    present = sum(there.astype(jnp.int32) for there, _ in greeted)
    pl.semaphore_wait(barrier, present)

    send(FIRST0, 1, faces0(pick_a), ghost_a)
    send(PROLONG0, 1, faces_p, ghosts_p)

    landed(prolong_one_ref, columns_one_ref, slots_one_ref, sends_one_ref)
    for g in range(4):
        for a in range(4):
            prolong1[pl.ds(16 * a + g, 4, 4), :] = prolong_one_ref[a, :, pl.ds(128 * g, 128)]
        index1[pl.ds(g, 7, 4), :] = columns_one_ref[:, pl.ds(128 * g, 128)]
        slot1[pl.ds(g, 7, 4), :] = slots_one_ref[:, pl.ds(128 * g, 128)]
    index1[28:32] = jnp.zeros((4, 128), jnp.int32)
    send1[...] = jnp.zeros((8, 128), jnp.int32)
    send1[0:3] = sends_one_ref[...]

    def pick1(table, pick, group):
        index = send1[...]
        [got] = lookup([index], [zeros], 0, 4, lambda c, j: table[pl.ds(4 * (4 * group + c) + j, 1), :])
        for c in range(4):
            for r in range(3):
                pick[r, pl.ds(4 * group + c, 1), :] = got[c][r:r + 1]

    def faces1(pick):
        return [pick.at[1], pick.at[0], pick.at[2], pick.at[2]]

    for group in range(4):
        pick1(prolong1, pick1_p, group)
    send(PROLONG1, 2, faces1(pick1_p), ghost1_p)

    landed(columns_ref, slots_ref, aggregates_ref)
    for j in range(16):
        turn[8 * j:8 * j + 7] = columns_ref[:, pl.ds(128 * j, 128)]
    for k in range(7):
        for h in range(2):
            index0[2 * k + h] = turn[pl.ds(64 * h + k, 8, 8), :]
    for j in range(16):
        turn[8 * j:8 * j + 7] = slots_ref[:, pl.ds(128 * j, 128)]
    for k in range(7):
        for h in range(2):
            slot0[2 * k + h] = turn[pl.ds(64 * h + k, 8, 8), :]

    def own0(v):
        got = lookup([index0[2 * v], index0[2 * v + 1]], (zeros,) * 2, 0, 16, table_row)
        for q in range(2):
            for c in range(4):
                near0[c, 2 * v + q] = got[q][c]

    def ghost0(ghost, v):
        held = [tuple(near0[c, 2 * v + q] for c in range(4)) for q in range(2)]
        got = lookup(
            [index0[2 * v], index0[2 * v + 1]], held, 16, 16, lambda c, j: ghost[j // 4, c, pl.ds(j % 4, 1), :]
        )
        for q in range(2):
            for c in range(4):
                near0[c, 2 * v + q] = got[q][c]

    def residual0(h):
        totals = []
        for a in range(4):
            def body(k, total):
                for c in range(4):
                    total = total + op0[16 * k + 4 * a + c, h] * near0[c, 2 * k + h]
                return total

            totals.append(src0[a, h] - loop(7, body, jnp.zeros((8, 128), F32)))
        return totals

    def each(count, function, unroll=True):
        def body(i, _):
            function(i)
            return 0

        lax.fori_loop(0, count, body, 0, unroll=unroll)

    each(7, own0, False)
    receive(FIRST0, 1, faces0(pick_a), ghost_a)
    each(7, lambda v: ghost0(ghost_a, v), False)
    for h in range(2):
        rest = residual0(h)
        for a in range(4):
            value = table0[a, h] + rest[a] / weight0[a, h]
            table0[a, h] = value
            result_ref[pl.ds(32 * h + a, 8, 4), :] = value
    pick0(table_row, 0, keep_in(pick_b))
    send(SECOND0, 1, faces0(pick_b), ghost_b)

    for j in range(16):
        rows = lax.broadcasted_iota(jnp.int32, (256, 128), 0)
        member0[:, pl.ds(128 * j, 128)] = jnp.where(
            rows == aggregates_ref[j:j + 1, :], 1.0, 0.0
        ).astype(BF16)
    for j in range(16):
        rows = pl.ds(16 * (j // 2), 16)
        for c in range(4):
            table_p[pl.ds(16 * (j // 2) + 4 * c, 4), pl.ds(128 * (j % 2), 128)] = prolong_ref[c, 4 * j:4 * j + 4, :]
    receive(PROLONG0, 1, faces_p, ghosts_p)
    for j in range(16):
        rows = pl.ds(128 + 16 * (j // 2), 16)
        table_p[rows, pl.ds(128 * (j % 2), 128)] = ghost_p[16 * j:16 * j + 16]
    high, low = split(table_p[...])
    terms_p[0:256] = high
    terms_p[256:512] = low

    def blocks_near(k):
        own0(k)
        index = columns_ref[pl.ds(k, 1), :]
        within = index & 255
        group = index >> 8
        rows = lax.broadcasted_iota(jnp.int32, (256, 2048), 0)
        chosen = jnp.where(rows == within, 1.0, 0.0).astype(BF16)
        both = jnp.dot(terms_p[...], chosen, preferred_element_type=F32)
        found = jnp.zeros((16, 2048), F32)
        for g in range(16):
            found = jnp.where(group == g, both[16 * g:16 * g + 16] + both[256 + 16 * g:272 + 16 * g], found)
        for j in range(16):
            nearp0[pl.ds(pl.multiple_of(256 * k + 16 * j, 8), 16), :] = found[:, 128 * j:128 * j + 128]

    each(7, blocks_near)

    def product0(v):
        k, h = v >> 1, v & 1
        for d in range(4):
            near = [nearp0[pl.ds(128 * v + 4 * c + d, 8, 16), :] for c in range(4)]
            inner = []
            for a in range(4):
                total = op0[16 * k + 4 * a, h] * near[0]
                for c in range(1, 4):
                    total = total + op0[16 * k + 4 * a + c, h] * near[c]
                inner.append(total)
            for b in range(4):
                total = prolong0[b, h] * inner[0]
                for a in range(1, 4):
                    total = total + prolong0[4 * a + b, h] * inner[a]
                blocks0[v, 4 * b + d] = total

    each(14, product0, False)

    def gather_slots0(bd):
        for h in range(2):
            gather_half0(bd, h)

    def gather_half0(bd, h):
        blocks = [blocks0[2 * k + h, bd] for k in range(7)]
        slots = [slot0[2 * k + h] for k in range(7)]
        for s in range(7):
            total = jnp.zeros((8, 128), F32)
            for k in range(7):
                total = total + jnp.where(slots[k] == s, blocks[k], 0.0)
            parts0[pl.ds(pl.multiple_of(256 * s + 16 * bd + 8 * h, 8), 8), :] = total

    each(16, gather_slots0, False)
    for j in range(16):
        high, low = split(parts0[pl.ds(j, 112, 16), :])
        left0[0:112, pl.ds(128 * j, 128)] = high
        left0[112:224, pl.ds(128 * j, 128)] = low
    both = against(left0[...], member0[...])
    coarse = both[0:112] + both[112:224]
    half = pl.multiple_of(224 * parity, 8)
    for jj in range(2):
        op1[pl.ds(half + 112 * jj, 112), :] = coarse[:, 128 * jj:128 * jj + 128]

    partner = (sub + 1 - 2 * parity, slab)
    mate = (sub + 2 - 4 * quad, slab)
    op1_half = op1.at[pl.ds(half, 224), :]
    op1_other = op1.at[pl.ds(pl.multiple_of(224 - 224 * parity, 8), 224), :]
    copy(OP1, 0, op1_half, op1_half, partner).start()

    receive(SECOND0, 1, faces0(pick_b), ghost_b)
    each(7, lambda v: ghost0(ghost_b, v), False)
    for h in range(2):
        rest = residual0(h)
        for b in range(4):
            total = prolong0[b, h] * rest[0]
            for a in range(1, 4):
                total = total + prolong0[4 * a + b, h] * rest[a]
            lifted0[pl.ds(32 * h + b, 8, 4), :] = total
    for j in range(16):
        value = lifted0[4 * j:4 * j + 4]
        lifted0w[0:4, pl.ds(128 * j, 128)] = value
        lifted0w[4:8, pl.ds(128 * j, 128)] = value - value.astype(BF16).astype(F32)
    both = against(lifted0w[...].astype(BF16), member0[...])
    coarse = both[0:4] + both[4:8]
    for jj in range(2):
        src1[2 * parity + jj] = coarse[:, 128 * jj:128 * jj + 128]
    src1_half = src1.at[pl.ds(2 * parity, 2)]
    src1_other = src1.at[pl.ds(2 - 2 * parity, 2)]
    copy(SRC1, 0, src1_half, src1_half, partner).start()

    def tiles1(pair):
        return [index1[16 * pair + 8 * v:16 * pair + 8 * v + 8] for v in range(2)]

    def own1(table, near, group):
        for pair in range(2):
            got = lookup(tiles1(pair), (zeros,) * 2, 0, 4, lambda c, j: table[pl.ds(4 * (4 * group + c) + j, 1), :])
            for v in range(2):
                for c in range(4):
                    near[4 * group + c, 16 * pair + 8 * v:16 * pair + 8 * v + 8, :] = got[v][c]

    upper_lanes = lax.broadcasted_iota(jnp.int32, (1, 128), 1) >= 64

    def ghost1(ghost, near, group):
        def last(c, j):
            channel = pl.ds(4 * group + c, 1)
            return jnp.where(upper_lanes, ghost[2, channel, :], ghost[3, channel, :])

        for pair in range(2):
            places = [pl.ds(16 * pair + 8 * v, 8) for v in range(2)]
            got = [tuple(near[4 * group + c, place, :] for c in range(4)) for place in places]
            got = lookup(tiles1(pair), got, 4, 2, lambda c, j: ghost[j, pl.ds(4 * group + c, 1), :])
            got = lookup(tiles1(pair), got, 6, 1, last, flip=64)
            for v in range(2):
                for c in range(4):
                    near[4 * group + c, places[v], :] = got[v][c]

    copy(OP1, 0, op1_half, op1_other, partner).wait_recv()

    def block1(k, a, c):
        return op1[pl.ds(16 * k + 4 * a + c, 4, 112), :]

    weight1 = []
    for a in range(4):
        def body(k, total):
            for c in range(4):
                total = total + jnp.abs(block1(k, a, c))
            return total

        weight1.append(loop(7, body, jnp.ones((4, 128), F32)))

    copy(SRC1, 0, src1_half, src1_other, partner).wait_recv()

    source1 = []
    first1 = []
    for a in range(4):
        source1.append(jnp.concatenate([src1[g, a:a + 1, :] for g in range(4)], axis=0))
        first1.append(source1[a] / weight1[a])
        table1[4 * a:4 * a + 4] = first1[a]
    pick1(table1, pick1_a, 0)
    send(FIRST1, 2, faces1(pick1_a), ghost1_a)
    own1(table1, near1, 0)

    each(4, lambda i: own1(prolong1, nearp1, i), False)
    receive(PROLONG1, 2, faces1(pick1_p), ghost1_p)
    each(4, lambda i: ghost1(ghost1_p, nearp1, i), False)
    landed(aggregates_one_ref, columns_two_ref, sends_two_ref)
    for g in range(4):
        rows = lax.broadcasted_iota(jnp.int32, (128, 128), 0)
        member1[:, pl.ds(128 * g, 128)] = jnp.where(
            rows == aggregates_one_ref[g:g + 1, :] + 64 * quad, 1.0, 0.0
        ).astype(BF16)

    def product1(k):
        for d in range(4):
            near = [nearp1[4 * c + d, pl.ds(4 * k, 4), :] for c in range(4)]
            inner = []
            for a in range(4):
                total = block1(k, a, 0) * near[0]
                for c in range(1, 4):
                    total = total + block1(k, a, c) * near[c]
                inner.append(total)
            for b in range(4):
                total = prolong1[4 * b:4 * b + 4] * inner[0]
                for a in range(1, 4):
                    total = total + prolong1[16 * a + 4 * b:16 * a + 4 * b + 4] * inner[a]
                blocks1[k, 4 * b + d] = total

    each(7, product1, False)

    def gather_slots1(bd):
        blocks = [blocks1[k, bd] for k in range(7)]
        slots = [slot1[4 * k:4 * k + 4] for k in range(7)]
        for s in range(7):
            total = jnp.zeros((4, 128), F32)
            for k in range(7):
                total = total + jnp.where(slots[k] == s, blocks[k], 0.0)
            parts1[16 * s + bd] = total

    each(16, gather_slots1, False)
    for g in range(4):
        high, low = split(parts1[:, g, :])
        left1[0:112, pl.ds(128 * g, 128)] = high
        left1[112:224, pl.ds(128 * g, 128)] = low
    both = against(left1[...], member1[...])
    op2[...] = both[0:112] + both[112:224]
    copy(OP2, 0, op2, op2x, mate).start()

    def residual1():
        totals = []
        for a in range(4):
            def body(k, total):
                for c in range(4):
                    total = total + block1(k, a, c) * near1[c, pl.ds(4 * k, 4), :]
                return total

            totals.append(source1[a] - loop(7, body, jnp.zeros((4, 128), F32)))
        return totals

    receive(FIRST1, 2, faces1(pick1_a), ghost1_a)
    ghost1(ghost1_a, near1, 0)
    rest = residual1()
    for a in range(4):
        value = first1[a] + rest[a] / weight1[a]
        table1[4 * a:4 * a + 4] = value
        x1[pl.ds(a, 4, 4), :] = value
    pick1(table1, pick1_b, 0)
    send(SECOND1, 2, faces1(pick1_b), ghost1_b)
    own1(table1, near1, 0)
    for jj in range(2):
        result_ref[64 + 4 * jj:68 + 4 * jj, :] = jnp.where(
            parity == 0, x1[4 * jj:4 * jj + 4], x1[8 + 4 * jj:12 + 4 * jj]
        )
    copy(OP2, 0, op2, op2x, mate).wait_recv()
    copy(OP2, 0, op2, op2x, mate).wait_send()
    op2[...] = op2[...] + op2x[...]
    block2 = [[op2[pl.ds(4 * a + c, 7, 16), :] for c in range(4)] for a in range(4)]
    weight2 = []
    for a in range(4):
        total = jnp.abs(block2[a][0])
        for c in range(1, 4):
            total = total + jnp.abs(block2[a][c])
        weight2.append(1.0 + jnp.sum(total, axis=0, keepdims=True))

    receive(SECOND1, 2, faces1(pick1_b), ghost1_b)
    ghost1(ghost1_b, near1, 0)
    rest = residual1()
    for b in range(4):
        total = prolong1[4 * b:4 * b + 4] * rest[0]
        for a in range(1, 4):
            total = total + prolong1[16 * a + 4 * b:16 * a + 4 * b + 4] * rest[a]
        lifted1[pl.ds(b, 4, 4), :] = total
    for g in range(4):
        value = lifted1[4 * g:4 * g + 4]
        lifted1w[0:4, pl.ds(128 * g, 128)] = value
        lifted1w[4:8, pl.ds(128 * g, 128)] = value - value.astype(BF16).astype(F32)
    both = against(lifted1w[...].astype(BF16), member1[...])
    src2[...] = both[0:4] + both[4:8]
    copy(SRC2, 0, src2, src2x, mate).start()

    index = columns_two_ref[...]
    lane = lax.broadcasted_iota(jnp.int32, (1, 128), 1)
    copy(SRC2, 0, src2, src2x, mate).wait_recv()
    source2 = src2[...] + src2x[...]
    first2 = [source2[a:a + 1] / weight2[a] for a in range(4)]
    wide = tuple(jnp.zeros((7, 128), F32) for _ in range(4))
    faces_row = jnp.reshape(sends_two_ref[0:128], (1, 128))
    sides_row = jnp.reshape(sends_two_ref[32:160], (1, 128))
    [picks] = lookup(
        [jnp.broadcast_to(faces_row, (8, 128))], [zeros], 0, 1, lambda c, j: first2[c]
    )
    for c in range(4):
        pick2[0, c:c + 1] = picks[c][0:1]
    [picks] = lookup(
        [jnp.broadcast_to(sides_row, (8, 128))], [zeros], 0, 1, lambda c, j: first2[c]
    )
    for c in range(4):
        pick2[1, c:c + 1] = picks[c][0:1]
    faces2 = [pick2.at[0], pick2.at[0], pick2.at[1], pick2.at[1]]
    send(FIRST2, 4, faces2, ghost2)
    near = lookup([index], [wide], 0, 1, lambda c, j: first2[c])
    receive(FIRST2, 4, faces2, ghost2)
    near = lookup(
        [index], near, 1, 1, lambda c, j: jnp.where(lane >= 64, ghost2[0, c:c + 1], ghost2[1, c:c + 1]), flip=64
    )
    [near] = lookup(
        [index], near, 2, 1, lambda c, j: jnp.where(lane >= 112, ghost2[2, c:c + 1], ghost2[3, c:c + 1]), flip=112
    )
    place = lax.rem(sub, 4)
    for a in range(4):
        total = block2[a][0] * near[0]
        for c in range(1, 4):
            total = total + block2[a][c] * near[c]
        rest2 = source2[a:a + 1] - jnp.sum(total, axis=0, keepdims=True)
        value = first2[a] + rest2 / weight2[a]
        share = value[:, 0:32]
        for q in range(1, 4):
            share = jnp.where(place == q, value[:, 32 * q:32 * q + 32], share)
        result_ref[72 + a:73 + a, 0:32] = share

    finish(FIRST0, 1, faces0(pick_a), ghost_a)
    finish(PROLONG0, 1, faces_p, ghosts_p)
    finish(PROLONG1, 2, faces1(pick1_p), ghost1_p)
    finish(SECOND0, 1, faces0(pick_b), ghost_b)
    finish(FIRST1, 2, faces1(pick1_a), ghost1_a)
    finish(SECOND1, 2, faces1(pick1_b), ghost1_b)
    finish(FIRST2, 4, faces2, ghost2)
    copy(OP1, 0, op1_half, op1_half, partner).wait_send()
    copy(SRC1, 0, src1_half, src1_half, partner).wait_send()
    copy(SRC2, 0, src2, src2x, mate).wait_send()


def fanout(result_ref, fine_ref, one_ref, two_ref):
    fine_ref[...] = result_ref[0:64]
    one_ref[...] = result_ref[64:72]
    two_ref[...] = result_ref[72:76, 0:32]


def fold(array):
    lead = array.shape[:-2]
    shaped = array.reshape(lead + (array.shape[-2], 16, 128))
    return jnp.swapaxes(shaped, -3, -2).reshape(lead + (16 * array.shape[-2], 128))


def on_device(
    source, operator, prolong, columns, slots, aggregates, sends,
    prolong_one, columns_one, slots_one, aggregates_one, sends_one, columns_two, sends_two,
):
    vmem = pl.BlockSpec(memory_space=pltpu.VMEM)
    landing = [
        ((64, 128), F32), ((28, 64, 128), F32), ((4, 64, 128), F32), ((7, 2048), jnp.int32), ((7, 2048), jnp.int32),
        ((16, 128), jnp.int32), ((16, 128), jnp.int32), ((4, 4, 512), F32), ((7, 512), jnp.int32),
        ((7, 512), jnp.int32), ((4, 128), jnp.int32), ((3, 128), jnp.int32), ((7, 128), jnp.int32),
        ((160,), jnp.int32),
    ]
    scratch = landing + [
        ((128, 128), jnp.int32), ((14, 8, 128), jnp.int32), ((14, 8, 128), jnp.int32),
        ((112, 2, 8, 128), F32), ((4, 2, 8, 128), F32), ((4, 2, 8, 128), F32), ((4, 2, 8, 128), F32),
        ((16, 2, 8, 128), F32), ((4, 14, 8, 128), F32), ((1792, 128), F32),
        ((14, 16, 8, 128), F32), ((1792, 128), F32), ((224, 2048), BF16), ((256, 2048), BF16),
        ((64, 128), F32), ((8, 2048), F32),
        ((4, 4, 4, 128), F32), ((4, 4, 4, 128), F32), ((256, 128), F32),
        ((4, 4, 4, 128), F32), ((4, 4, 4, 128), F32), ((256, 128), F32),
        ((448, 128), F32), ((4, 4, 128), F32), ((32, 128), jnp.int32), ((32, 128), jnp.int32),
        ((64, 128), F32), ((16, 128), F32), ((4, 32, 128), F32), ((16, 32, 128), F32),
        ((7, 16, 4, 128), F32), ((112, 4, 128), F32), ((224, 512), BF16), ((128, 512), BF16),
        ((16, 128), F32), ((8, 512), F32), ((16, 128), F32), ((8, 128), jnp.int32),
        ((3, 16, 128), F32), ((3, 4, 128), F32), ((3, 4, 128), F32),
        ((4, 16, 128), F32), ((4, 4, 128), F32), ((4, 4, 128), F32),
        ((112, 128), F32), ((112, 128), F32), ((4, 128), F32), ((4, 128), F32),
        ((2, 4, 128), F32), ((4, 4, 128), F32), ((256, 256), F32), ((512, 256), BF16),
    ]
    result = pl.pallas_call(
        kernel,
        out_shape=jax.ShapeDtypeStruct((80, 128), F32),
        in_specs=[pl.BlockSpec(memory_space=pl.ANY)] * 14,
        out_specs=vmem,
        scratch_shapes=[pltpu.VMEM(shape, kind) for shape, kind in scratch]
        + [pltpu.SemaphoreType.DMA(shape) for shape in ((14,), (11, 4), (11, 4))],
        compiler_params=pltpu.CompilerParams(
            collective_id=0, has_side_effects=True, vmem_limit_bytes=60 << 20
        ),
        name="descend",
    )(
        fold(source), fold(operator).reshape(28, 64, 128), fold(prolong), columns, slots,
        aggregates.reshape(16, 128), sends.reshape(16, 128),
        prolong_one, columns_one, slots_one, aggregates_one.reshape(4, 128), sends_one.reshape(3, 128),
        columns_two, sends_two,
    )
    shares = pl.pallas_call(
        fanout,
        out_shape=[jax.ShapeDtypeStruct(shape, F32) for shape in ((64, 128), (8, 128), (4, 32))],
        in_specs=[vmem],
        out_specs=[vmem] * 3,
        name="fanout",
    )(result)

    def unfold(rows):
        return rows.reshape(-1, 4, 128).swapaxes(0, 1).reshape(4, -1)

    return unfold(shares[0]), unfold(shares[1]), shares[2]


def solution(mesh):
    both = ("sub", "slab")
    flat = P(both)
    rows = P(None, both)
    blocks = P(None, None, both)
    placed = (
        rows, P(None, None, None, both), blocks, rows, rows, flat, flat,
        blocks, rows, rows, flat, flat, rows, flat,
    )
    return jax.shard_map(
        on_device, mesh=mesh, in_specs=placed, out_specs=(rows, rows, rows), check_vma=False
    )
```

```python
import jax
import jax.numpy as jnp
from jax import lax
from jax.experimental import pallas as pl
from jax.experimental.pallas import tpu as pltpu
from jax.sharding import PartitionSpec as P

F32 = jnp.float32
BF16 = jnp.bfloat16
MESH = pl.DeviceIdType.MESH

FIRST0, SECOND0, PROLONG0, PROLONG1, FIRST1, SECOND1, FIRST2, OP1, SRC1, OP2, SRC2, CROSS2 = range(12)


def loop(count, body, init=0):
    return lax.fori_loop(0, count, body, init, unroll=True)


LANES = lax.GatherDimensionNumbers(
    offset_dims=(), collapsed_slice_dims=(1,), start_index_map=(1,),
    operand_batching_dims=(0,), start_indices_batching_dims=(0,),
)


def pick_lanes(values, lanes):
    return lax.gather(
        values, lanes[..., None], LANES, slice_sizes=(1, 1), mode=lax.GatherScatterMode.PROMISE_IN_BOUNDS
    )


def lookup(indices, init, base, count, row, flip=0):
    lanes = [(index & 127) ^ flip if flip else index & 127 for index in indices]
    highs = [index >> 7 for index in indices]
    channels = len(init[0])

    held = [list(tile) for tile in init]
    for j in range(count):
        here = [high == base + j for high in highs]
        for c in range(channels):
            spread = jnp.broadcast_to(row(c, j), indices[0].shape)
            for v, lane in enumerate(lanes):
                held[v][c] = jnp.where(here[v], pick_lanes(spread, lane), held[v][c])
    return held


def split(value):
    high = value.astype(BF16)
    return high, (value - high.astype(F32)).astype(BF16)


def against(left, right):
    return lax.dot_general(left, right, (((1,), (1,)), ((), ())), preferred_element_type=F32)


def kernel(
    source_in, operator_in, prolong_in, columns_in, slots_in, aggregates_in, sends_in,
    prolong_one_in, columns_one_in, slots_one_in, aggregates_one_in, sends_one_in,
    columns_two_in, sends_two_in,
    result_ref,
    source_ref, operator_ref, prolong_ref, columns_ref, slots_ref, aggregates_ref, sends_ref,
    prolong_one_ref, columns_one_ref, slots_one_ref, aggregates_one_ref, sends_one_ref,
    columns_two_ref, sends_two_ref,
    turn, index0, slot0, op0, src0, weight0, table0, prolong0, near0, nearp0, blocks0, parts0,
    left0, member0, lifted0, lifted0w, pick_a, pick_b, pick_p, ghost_a, ghost_b, ghost_p,
    op1, src1, index1, slot1, prolong1, table1, near1, nearp1, blocks1, parts1, left1, member1,
    lifted1, lifted1w, x1, send1, pick1_p, pick1_a, pick1_b, ghost1_p, ghost1_a, ghost1_b,
    op2, op2x, src2, src2x, pick2, ghost2, cross2, table_p, terms_p, load_sem, send_sem, recv_sem,
):
    inputs = [
        (sends_in, sends_ref), (prolong_in, prolong_ref), (source_in, source_ref), (operator_in, operator_ref),
        (columns_in, columns_ref), (prolong_one_in, prolong_one_ref), (sends_one_in, sends_one_ref),
        (aggregates_in, aggregates_ref), (slots_in, slots_ref), (columns_one_in, columns_one_ref),
        (slots_one_in, slots_one_ref), (aggregates_one_in, aggregates_one_ref),
        (columns_two_in, columns_two_ref), (sends_two_in, sends_two_ref),
    ]
    loads = {
        id(place): pltpu.make_async_copy(given, place, load_sem.at[i]) for i, (given, place) in enumerate(inputs)
    }
    for _, place in inputs:
        loads[id(place)].start()

    def landed(*places):
        for place in places:
            loads[id(place)].wait()

    sub = lax.axis_index("sub")
    slab = lax.axis_index("slab")
    n_sub = lax.axis_size("sub")
    n_slab = lax.axis_size("slab")
    parity = lax.rem(sub, 2)
    quad = lax.rem(sub // 2, 2)
    has_before = slab > 0
    has_after = slab < n_slab - 1

    barrier = pltpu.get_barrier_semaphore()
    greeted = [(has_before, (sub, slab - 1)), (has_after, (sub, slab + 1))]
    for far in (1, 2, 4):
        greeted += [(sub >= far, (sub - far, slab)), (sub < n_sub - far, (sub + far, slab))]
    across = 2 - 4 * quad
    greeted += [(has_before, (sub + across, slab - 1)), (has_after, (sub + across, slab + 1))]
    greeted += [
        (jnp.logical_and(quad == 0, sub < n_sub - 4), (sub + 6, slab)),
        (jnp.logical_and(quad == 1, sub >= 4), (sub - 6, slab)),
    ]
    for there, peer in greeted:
        @pl.when(there)
        def _(peer=peer):
            pl.semaphore_signal(barrier, inc=1, device_id=peer, device_id_type=MESH)

    def routes(far, shift=0):
        after = (has_after, (sub + shift, slab + 1))
        before = (has_before, (sub + shift, slab - 1))
        upper = (sub < n_sub - far, (sub + far + shift, slab))
        lower = (sub >= far, (sub - far + shift, slab))
        return [(after, before), (before, after), (upper, lower), (lower, upper)]

    def copy(name, d, piece, ghost, peer):
        return pltpu.make_async_remote_copy(
            piece, ghost, send_sem.at[name, d], recv_sem.at[name, d], device_id=peer, device_id_type=MESH
        )

    def part(ghost, d):
        return ghost[d] if isinstance(ghost, list) else ghost.at[d]

    def send(name, far, pieces, ghost, shift=0):
        for d, (to, _) in enumerate(routes(far, shift)):
            @pl.when(to[0])
            def _(d=d, to=to):
                copy(name, d, pieces[d], part(ghost, d), to[1]).start()

    def receive(name, far, pieces, ghost, shift=0):
        for d, (_, source) in enumerate(routes(far, shift)):
            @pl.when(source[0])
            def _(d=d, source=source):
                copy(name, d, pieces[d], part(ghost, d), source[1]).wait_recv()

    def finish(name, far, pieces, ghost, shift=0):
        for d, (to, _) in enumerate(routes(far, shift)):
            @pl.when(to[0])
            def _(d=d, to=to):
                copy(name, d, pieces[d], part(ghost, d), to[1]).wait_send()

    def clear(far, ghosts):
        for d, (_, source) in enumerate(routes(far)):
            @pl.when(jnp.logical_not(source[0]))
            def _(d=d):
                for ghost in ghosts:
                    ghost[d] = jnp.zeros_like(ghost[d])

    clear(1, (ghost_a, ghost_b))
    for d, (_, giver) in enumerate(routes(1)):
        @pl.when(jnp.logical_not(giver[0]))
        def _(d=d):
            ghost_p[64 * d:64 * d + 64] = jnp.zeros((64, 128), F32)
    clear(2, (ghost1_a, ghost1_b, ghost1_p))
    clear(4, (ghost2, cross2))

    zeros = tuple(jnp.zeros((8, 128), F32) for _ in range(4))

    def pick0(row, group, keep):
        got = lookup([sends_ref[0:8, :], sends_ref[8:16, :]], (zeros,) * 2, 0, 16, lambda c, j: row(4 * group + c, j))
        for h in range(2):
            for c in range(4):
                keep(h, 4 * group + c, got[h][c])

    def keep_in(pick):
        def keep(h, c, got):
            pick[2 * h, c] = got[0:4]
            pick[2 * h + 1, c] = got[4:8]

        return keep

    def keep_prolong(h, c, got):
        pick_p[pl.ds(128 * h + c, 8, 16), :] = got

    def table_row(c, j):
        return table0[c, j // 8, pl.ds(j % 8, 1), :]

    def faces0(pick):
        return [pick.at[1], pick.at[0], pick.at[3], pick.at[2]]

    faces_p = [pick_p.at[pl.ds(64 * d, 64), :] for d in (1, 0, 3, 2)]
    ghosts_p = [ghost_p.at[pl.ds(64 * d, 64), :] for d in range(4)]

    landed(sends_ref, prolong_ref)

    def spread_prolong(a, _):
        for h in range(2):
            for b in range(4):
                prolong0[4 * a + b, h] = prolong_ref[a, pl.ds(32 * h + b, 8, 4), :]
        return 0

    lax.fori_loop(0, 4, spread_prolong, 0, unroll=True)

    def pick_prolong(group, _):
        pick0(lambda c, j: prolong0[c, j // 8, pl.ds(j % 8, 1), :], group, keep_prolong)
        return 0

    lax.fori_loop(0, 4, pick_prolong, 0, unroll=True)

    landed(source_ref, operator_ref)
    for h in range(2):
        for a in range(4):
            src0[a, h] = source_ref[pl.ds(32 * h + a, 8, 4), :]

    def weigh(a, _):
        for h in range(2):
            def slot_body(k, total):
                for c in range(4):
                    value = operator_ref[4 * k + a, pl.ds(32 * h + c, 8, 4), :]
                    op0[16 * k + 4 * a + c, h] = value
                    total = total + jnp.abs(value)
                return total

            total = loop(7, slot_body, jnp.ones((8, 128), F32))
            weight0[a, h] = total
            table0[a, h] = src0[a, h] / total
        return 0

    lax.fori_loop(0, 4, weigh, 0, unroll=True)
    pick0(table_row, 0, keep_in(pick_a))

    present = sum(there.astype(jnp.int32) for there, _ in greeted)
    pl.semaphore_wait(barrier, present)

    send(FIRST0, 1, faces0(pick_a), ghost_a)
    send(PROLONG0, 1, faces_p, ghosts_p)

    landed(prolong_one_ref, columns_one_ref, slots_one_ref, sends_one_ref)
    for g in range(4):
        for a in range(4):
            prolong1[pl.ds(16 * a + g, 4, 4), :] = prolong_one_ref[a, :, pl.ds(128 * g, 128)]
        index1[pl.ds(g, 7, 4), :] = columns_one_ref[:, pl.ds(128 * g, 128)]
        slot1[pl.ds(g, 7, 4), :] = slots_one_ref[:, pl.ds(128 * g, 128)]
    index1[28:32] = jnp.zeros((4, 128), jnp.int32)
    send1[...] = jnp.zeros((8, 128), jnp.int32)
    send1[0:3] = sends_one_ref[...]

    def pick1(table, pick, group):
        index = send1[...]
        [got] = lookup([index], [zeros], 0, 4, lambda c, j: table[pl.ds(4 * (4 * group + c) + j, 1), :])
        for c in range(4):
            for r in range(3):
                pick[r, pl.ds(4 * group + c, 1), :] = got[c][r:r + 1]

    def faces1(pick):
        return [pick.at[1], pick.at[0], pick.at[2], pick.at[2]]

    for group in range(4):
        pick1(prolong1, pick1_p, group)
    send(PROLONG1, 2, faces1(pick1_p), ghost1_p)

    landed(columns_ref, slots_ref, aggregates_ref)
    for j in range(16):
        turn[8 * j:8 * j + 7] = columns_ref[:, pl.ds(128 * j, 128)]
    for k in range(7):
        for h in range(2):
            index0[2 * k + h] = turn[pl.ds(64 * h + k, 8, 8), :]
    for j in range(16):
        turn[8 * j:8 * j + 7] = slots_ref[:, pl.ds(128 * j, 128)]
    for k in range(7):
        for h in range(2):
            slot0[2 * k + h] = turn[pl.ds(64 * h + k, 8, 8), :]

    def own0(v):
        got = lookup([index0[2 * v], index0[2 * v + 1]], (zeros,) * 2, 0, 16, table_row)
        for q in range(2):
            for c in range(4):
                near0[c, 2 * v + q] = got[q][c]

    def ghost0(ghost, v):
        held = [tuple(near0[c, 2 * v + q] for c in range(4)) for q in range(2)]
        got = lookup(
            [index0[2 * v], index0[2 * v + 1]], held, 16, 16, lambda c, j: ghost[j // 4, c, pl.ds(j % 4, 1), :]
        )
        for q in range(2):
            for c in range(4):
                near0[c, 2 * v + q] = got[q][c]

    def residual0(h):
        totals = []
        for a in range(4):
            def body(k, total):
                for c in range(4):
                    total = total + op0[16 * k + 4 * a + c, h] * near0[c, 2 * k + h]
                return total

            totals.append(src0[a, h] - loop(7, body, jnp.zeros((8, 128), F32)))
        return totals

    def each(count, function, unroll=True):
        def body(i, _):
            function(i)
            return 0

        lax.fori_loop(0, count, body, 0, unroll=unroll)

    each(7, own0)
    receive(FIRST0, 1, faces0(pick_a), ghost_a)
    each(7, lambda v: ghost0(ghost_a, v))
    for h in range(2):
        rest = residual0(h)
        for a in range(4):
            value = table0[a, h] + rest[a] / weight0[a, h]
            table0[a, h] = value
            result_ref[pl.ds(32 * h + a, 8, 4), :] = value
    pick0(table_row, 0, keep_in(pick_b))
    send(SECOND0, 1, faces0(pick_b), ghost_b)

    for j in range(16):
        rows = lax.broadcasted_iota(jnp.int32, (256, 128), 0)
        member0[:, pl.ds(128 * j, 128)] = jnp.where(
            rows == aggregates_ref[j:j + 1, :], 1.0, 0.0
        ).astype(BF16)
    for j in range(16):
        rows = pl.ds(16 * (j // 2), 16)
        for c in range(4):
            table_p[pl.ds(16 * (j // 2) + 4 * c, 4), pl.ds(128 * (j % 2), 128)] = prolong_ref[c, 4 * j:4 * j + 4, :]
    receive(PROLONG0, 1, faces_p, ghosts_p)
    for j in range(16):
        rows = pl.ds(128 + 16 * (j // 2), 16)
        table_p[rows, pl.ds(128 * (j % 2), 128)] = ghost_p[16 * j:16 * j + 16]
    high, low = split(table_p[...])
    terms_p[0:256] = high
    terms_p[256:512] = low

    def blocks_near(k):
        own0(k)
        index = columns_ref[pl.ds(k, 1), :]
        within = index & 255
        group = index >> 8
        rows = lax.broadcasted_iota(jnp.int32, (256, 2048), 0)
        chosen = jnp.where(rows == within, 1.0, 0.0).astype(BF16)
        both = jnp.dot(terms_p[...], chosen, preferred_element_type=F32)
        found = jnp.zeros((16, 2048), F32)
        for g in range(16):
            found = jnp.where(group == g, both[16 * g:16 * g + 16] + both[256 + 16 * g:272 + 16 * g], found)
        for j in range(16):
            nearp0[pl.ds(pl.multiple_of(256 * k + 16 * j, 8), 16), :] = found[:, 128 * j:128 * j + 128]

    each(7, blocks_near)

    def product0(v):
        k, h = v >> 1, v & 1
        for d in range(4):
            near = [nearp0[pl.ds(128 * v + 4 * c + d, 8, 16), :] for c in range(4)]
            inner = []
            for a in range(4):
                total = op0[16 * k + 4 * a, h] * near[0]
                for c in range(1, 4):
                    total = total + op0[16 * k + 4 * a + c, h] * near[c]
                inner.append(total)
            for b in range(4):
                total = prolong0[b, h] * inner[0]
                for a in range(1, 4):
                    total = total + prolong0[4 * a + b, h] * inner[a]
                blocks0[v, 4 * b + d] = total

    each(14, product0, 2)

    def gather_slots0(bd):
        for h in range(2):
            gather_half0(bd, h)

    def gather_half0(bd, h):
        blocks = [blocks0[2 * k + h, bd] for k in range(7)]
        slots = [slot0[2 * k + h] for k in range(7)]
        for s in range(7):
            total = jnp.zeros((8, 128), F32)
            for k in range(7):
                total = total + jnp.where(slots[k] == s, blocks[k], 0.0)
            parts0[pl.ds(pl.multiple_of(256 * s + 16 * bd + 8 * h, 8), 8), :] = total

    each(16, gather_slots0, False)
    for j in range(16):
        high, low = split(parts0[pl.ds(j, 112, 16), :])
        left0[0:112, pl.ds(128 * j, 128)] = high
        left0[112:224, pl.ds(128 * j, 128)] = low
    both = against(left0[...], member0[...])
    coarse = both[0:112] + both[112:224]
    half = pl.multiple_of(224 * parity, 8)
    for jj in range(2):
        op1[pl.ds(half + 112 * jj, 112), :] = coarse[:, 128 * jj:128 * jj + 128]

    partner = (sub + 1 - 2 * parity, slab)
    mate = (sub + 2 - 4 * quad, slab)
    op1_half = op1.at[pl.ds(half, 224), :]
    op1_other = op1.at[pl.ds(pl.multiple_of(224 - 224 * parity, 8), 224), :]
    copy(OP1, 0, op1_half, op1_half, partner).start()

    receive(SECOND0, 1, faces0(pick_b), ghost_b)
    each(7, lambda v: ghost0(ghost_b, v))
    for h in range(2):
        rest = residual0(h)
        for b in range(4):
            total = prolong0[b, h] * rest[0]
            for a in range(1, 4):
                total = total + prolong0[4 * a + b, h] * rest[a]
            lifted0[pl.ds(32 * h + b, 8, 4), :] = total
    for j in range(16):
        value = lifted0[4 * j:4 * j + 4]
        lifted0w[0:4, pl.ds(128 * j, 128)] = value
        lifted0w[4:8, pl.ds(128 * j, 128)] = value - value.astype(BF16).astype(F32)
    both = against(lifted0w[...].astype(BF16), member0[...])
    coarse = both[0:4] + both[4:8]
    for jj in range(2):
        src1[2 * parity + jj] = coarse[:, 128 * jj:128 * jj + 128]
    src1_half = src1.at[pl.ds(2 * parity, 2)]
    src1_other = src1.at[pl.ds(2 - 2 * parity, 2)]
    copy(SRC1, 0, src1_half, src1_half, partner).start()

    def tiles1(pair):
        return [index1[16 * pair + 8 * v:16 * pair + 8 * v + 8] for v in range(2)]

    def own1(table, near, group):
        for pair in range(2):
            got = lookup(tiles1(pair), (zeros,) * 2, 0, 4, lambda c, j: table[pl.ds(4 * (4 * group + c) + j, 1), :])
            for v in range(2):
                for c in range(4):
                    near[4 * group + c, 16 * pair + 8 * v:16 * pair + 8 * v + 8, :] = got[v][c]

    upper_lanes = lax.broadcasted_iota(jnp.int32, (1, 128), 1) >= 64

    def ghost1(ghost, near, group):
        def last(c, j):
            channel = pl.ds(4 * group + c, 1)
            return jnp.where(upper_lanes, ghost[2, channel, :], ghost[3, channel, :])

        for pair in range(2):
            places = [pl.ds(16 * pair + 8 * v, 8) for v in range(2)]
            got = [tuple(near[4 * group + c, place, :] for c in range(4)) for place in places]
            got = lookup(tiles1(pair), got, 4, 2, lambda c, j: ghost[j, pl.ds(4 * group + c, 1), :])
            got = lookup(tiles1(pair), got, 6, 1, last, flip=64)
            for v in range(2):
                for c in range(4):
                    near[4 * group + c, places[v], :] = got[v][c]

    copy(OP1, 0, op1_half, op1_other, partner).wait_recv()

    def block1(k, a, c):
        return op1[pl.ds(16 * k + 4 * a + c, 4, 112), :]

    weight1 = []
    for a in range(4):
        def body(k, total):
            for c in range(4):
                total = total + jnp.abs(block1(k, a, c))
            return total

        weight1.append(loop(7, body, jnp.ones((4, 128), F32)))

    copy(SRC1, 0, src1_half, src1_other, partner).wait_recv()

    source1 = []
    first1 = []
    for a in range(4):
        source1.append(jnp.concatenate([src1[g, a:a + 1, :] for g in range(4)], axis=0))
        first1.append(source1[a] / weight1[a])
        table1[4 * a:4 * a + 4] = first1[a]
    pick1(table1, pick1_a, 0)
    send(FIRST1, 2, faces1(pick1_a), ghost1_a)
    own1(table1, near1, 0)

    each(4, lambda i: own1(prolong1, nearp1, i), False)
    receive(PROLONG1, 2, faces1(pick1_p), ghost1_p)
    each(4, lambda i: ghost1(ghost1_p, nearp1, i), False)
    landed(aggregates_one_ref, columns_two_ref, sends_two_ref)
    for g in range(4):
        rows = lax.broadcasted_iota(jnp.int32, (128, 128), 0)
        member1[:, pl.ds(128 * g, 128)] = jnp.where(
            rows == aggregates_one_ref[g:g + 1, :] + 64 * quad, 1.0, 0.0
        ).astype(BF16)

    def product1(k):
        for d in range(4):
            near = [nearp1[4 * c + d, pl.ds(4 * k, 4), :] for c in range(4)]
            inner = []
            for a in range(4):
                total = block1(k, a, 0) * near[0]
                for c in range(1, 4):
                    total = total + block1(k, a, c) * near[c]
                inner.append(total)
            for b in range(4):
                total = prolong1[4 * b:4 * b + 4] * inner[0]
                for a in range(1, 4):
                    total = total + prolong1[16 * a + 4 * b:16 * a + 4 * b + 4] * inner[a]
                blocks1[k, 4 * b + d] = total

    each(7, product1)

    def gather_slots1(bd):
        blocks = [blocks1[k, bd] for k in range(7)]
        slots = [slot1[4 * k:4 * k + 4] for k in range(7)]
        for s in range(7):
            total = jnp.zeros((4, 128), F32)
            for k in range(7):
                total = total + jnp.where(slots[k] == s, blocks[k], 0.0)
            parts1[16 * s + bd] = total

    each(16, gather_slots1)
    for g in range(4):
        high, low = split(parts1[:, g, :])
        left1[0:112, pl.ds(128 * g, 128)] = high
        left1[112:224, pl.ds(128 * g, 128)] = low
    both = against(left1[...], member1[...])
    op2[...] = both[0:112] + both[112:224]
    copy(OP2, 0, op2, op2x, mate).start()

    def residual1():
        totals = []
        for a in range(4):
            def body(k, total):
                for c in range(4):
                    total = total + block1(k, a, c) * near1[c, pl.ds(4 * k, 4), :]
                return total

            totals.append(source1[a] - loop(7, body, jnp.zeros((4, 128), F32)))
        return totals

    receive(FIRST1, 2, faces1(pick1_a), ghost1_a)
    ghost1(ghost1_a, near1, 0)
    rest = residual1()
    for a in range(4):
        value = first1[a] + rest[a] / weight1[a]
        table1[4 * a:4 * a + 4] = value
        x1[pl.ds(a, 4, 4), :] = value
    pick1(table1, pick1_b, 0)
    send(SECOND1, 2, faces1(pick1_b), ghost1_b)
    own1(table1, near1, 0)
    for jj in range(2):
        result_ref[64 + 4 * jj:68 + 4 * jj, :] = jnp.where(
            parity == 0, x1[4 * jj:4 * jj + 4], x1[8 + 4 * jj:12 + 4 * jj]
        )
    copy(OP2, 0, op2, op2x, mate).wait_recv()
    copy(OP2, 0, op2, op2x, mate).wait_send()
    op2[...] = op2[...] + op2x[...]
    block2 = [[op2[pl.ds(4 * a + c, 7, 16), :] for c in range(4)] for a in range(4)]
    weight2 = []
    for a in range(4):
        total = jnp.abs(block2[a][0])
        for c in range(1, 4):
            total = total + jnp.abs(block2[a][c])
        weight2.append(1.0 + jnp.sum(total, axis=0, keepdims=True))

    receive(SECOND1, 2, faces1(pick1_b), ghost1_b)
    ghost1(ghost1_b, near1, 0)
    rest = residual1()
    for b in range(4):
        total = prolong1[4 * b:4 * b + 4] * rest[0]
        for a in range(1, 4):
            total = total + prolong1[16 * a + 4 * b:16 * a + 4 * b + 4] * rest[a]
        lifted1[pl.ds(b, 4, 4), :] = total
    for g in range(4):
        value = lifted1[4 * g:4 * g + 4]
        lifted1w[0:4, pl.ds(128 * g, 128)] = value
        lifted1w[4:8, pl.ds(128 * g, 128)] = value - value.astype(BF16).astype(F32)
    both = against(lifted1w[...].astype(BF16), member1[...])
    half2 = both[0:4] + both[4:8]
    src2[0:4] = half2
    for a in range(4):
        src2[4 + a:5 + a] = half2[a:a + 1] / weight2[a]
    copy(SRC2, 0, src2, src2x, mate).start()

    faces_row = jnp.reshape(sends_two_ref[0:128], (1, 128))
    sides_row = jnp.reshape(sends_two_ref[32:160], (1, 128))
    for r, listed in enumerate((faces_row, sides_row)):
        [picks] = lookup(
            [jnp.broadcast_to(listed, (8, 128))], [zeros], 0, 1, lambda c, j: src2[4 + c:5 + c]
        )
        for c in range(4):
            pick2[r, c:c + 1] = picks[c][0:1]
    faces2 = [pick2.at[0], pick2.at[0], pick2.at[1], pick2.at[1]]
    send(FIRST2, 4, faces2, ghost2)
    send(CROSS2, 4, faces2, cross2, across)
    index = columns_two_ref[...]
    lane = lax.broadcasted_iota(jnp.int32, (1, 128), 1)
    wide = tuple(jnp.zeros((7, 128), F32) for _ in range(4))
    copy(SRC2, 0, src2, src2x, mate).wait_recv()
    whole2 = src2[...] + src2x[...]
    source2 = whole2[0:4]
    first2 = [whole2[4 + a:5 + a] for a in range(4)]
    near = lookup([index], [wide], 0, 1, lambda c, j: first2[c])
    receive(FIRST2, 4, faces2, ghost2)
    receive(CROSS2, 4, faces2, cross2, across)

    def ghost_row(d, c):
        return ghost2[d, c:c + 1] + cross2[d, c:c + 1]

    near = lookup(
        [index], near, 1, 1, lambda c, j: jnp.where(lane >= 64, ghost_row(0, c), ghost_row(1, c)), flip=64
    )
    [near] = lookup(
        [index], near, 2, 1, lambda c, j: jnp.where(lane >= 112, ghost_row(2, c), ghost_row(3, c)), flip=112
    )
    place = lax.rem(sub, 4)
    for a in range(4):
        total = block2[a][0] * near[0]
        for c in range(1, 4):
            total = total + block2[a][c] * near[c]
        rest2 = source2[a:a + 1] - jnp.sum(total, axis=0, keepdims=True)
        value = first2[a] + rest2 / weight2[a]
        share = value[:, 0:32]
        for q in range(1, 4):
            share = jnp.where(place == q, value[:, 32 * q:32 * q + 32], share)
        result_ref[72 + a:73 + a, 0:32] = share

    finish(FIRST0, 1, faces0(pick_a), ghost_a)
    finish(PROLONG0, 1, faces_p, ghosts_p)
    finish(PROLONG1, 2, faces1(pick1_p), ghost1_p)
    finish(SECOND0, 1, faces0(pick_b), ghost_b)
    finish(FIRST1, 2, faces1(pick1_a), ghost1_a)
    finish(SECOND1, 2, faces1(pick1_b), ghost1_b)
    finish(FIRST2, 4, faces2, ghost2)
    finish(CROSS2, 4, faces2, cross2, across)
    copy(OP1, 0, op1_half, op1_half, partner).wait_send()
    copy(SRC1, 0, src1_half, src1_half, partner).wait_send()
    copy(SRC2, 0, src2, src2x, mate).wait_send()


def fanout(result_ref, fine_ref, one_ref, two_ref):
    fine_ref[...] = result_ref[0:64]
    one_ref[...] = result_ref[64:72]
    two_ref[...] = result_ref[72:76, 0:32]


def fold(array):
    lead = array.shape[:-2]
    shaped = array.reshape(lead + (array.shape[-2], 16, 128))
    return jnp.swapaxes(shaped, -3, -2).reshape(lead + (16 * array.shape[-2], 128))


def on_device(
    source, operator, prolong, columns, slots, aggregates, sends,
    prolong_one, columns_one, slots_one, aggregates_one, sends_one, columns_two, sends_two,
):
    vmem = pl.BlockSpec(memory_space=pltpu.VMEM)
    landing = [
        ((64, 128), F32), ((28, 64, 128), F32), ((4, 64, 128), F32), ((7, 2048), jnp.int32), ((7, 2048), jnp.int32),
        ((16, 128), jnp.int32), ((16, 128), jnp.int32), ((4, 4, 512), F32), ((7, 512), jnp.int32),
        ((7, 512), jnp.int32), ((4, 128), jnp.int32), ((3, 128), jnp.int32), ((7, 128), jnp.int32),
        ((160,), jnp.int32),
    ]
    scratch = landing + [
        ((128, 128), jnp.int32), ((14, 8, 128), jnp.int32), ((14, 8, 128), jnp.int32),
        ((112, 2, 8, 128), F32), ((4, 2, 8, 128), F32), ((4, 2, 8, 128), F32), ((4, 2, 8, 128), F32),
        ((16, 2, 8, 128), F32), ((4, 14, 8, 128), F32), ((1792, 128), F32),
        ((14, 16, 8, 128), F32), ((1792, 128), F32), ((224, 2048), BF16), ((256, 2048), BF16),
        ((64, 128), F32), ((8, 2048), F32),
        ((4, 4, 4, 128), F32), ((4, 4, 4, 128), F32), ((256, 128), F32),
        ((4, 4, 4, 128), F32), ((4, 4, 4, 128), F32), ((256, 128), F32),
        ((448, 128), F32), ((4, 4, 128), F32), ((32, 128), jnp.int32), ((32, 128), jnp.int32),
        ((64, 128), F32), ((16, 128), F32), ((4, 32, 128), F32), ((16, 32, 128), F32),
        ((7, 16, 4, 128), F32), ((112, 4, 128), F32), ((224, 512), BF16), ((128, 512), BF16),
        ((16, 128), F32), ((8, 512), F32), ((16, 128), F32), ((8, 128), jnp.int32),
        ((3, 16, 128), F32), ((3, 4, 128), F32), ((3, 4, 128), F32),
        ((4, 16, 128), F32), ((4, 4, 128), F32), ((4, 4, 128), F32),
        ((112, 128), F32), ((112, 128), F32), ((8, 128), F32), ((8, 128), F32),
        ((2, 4, 128), F32), ((4, 4, 128), F32), ((4, 4, 128), F32), ((256, 256), F32), ((512, 256), BF16),
    ]
    result = pl.pallas_call(
        kernel,
        out_shape=jax.ShapeDtypeStruct((80, 128), F32),
        in_specs=[pl.BlockSpec(memory_space=pl.ANY)] * 14,
        out_specs=vmem,
        scratch_shapes=[pltpu.VMEM(shape, kind) for shape, kind in scratch]
        + [pltpu.SemaphoreType.DMA(shape) for shape in ((14,), (12, 4), (12, 4))],
        compiler_params=pltpu.CompilerParams(
            collective_id=0, has_side_effects=True, vmem_limit_bytes=60 << 20
        ),
        name="descend",
    )(
        fold(source), fold(operator).reshape(28, 64, 128), fold(prolong), columns, slots,
        aggregates.reshape(16, 128), sends.reshape(16, 128),
        prolong_one, columns_one, slots_one, aggregates_one.reshape(4, 128), sends_one.reshape(3, 128),
        columns_two, sends_two,
    )
    shares = pl.pallas_call(
        fanout,
        out_shape=[jax.ShapeDtypeStruct(shape, F32) for shape in ((64, 128), (8, 128), (4, 32))],
        in_specs=[vmem],
        out_specs=[vmem] * 3,
        name="fanout",
    )(result)

    def unfold(rows):
        return rows.reshape(-1, 4, 128).swapaxes(0, 1).reshape(4, -1)

    return unfold(shares[0]), unfold(shares[1]), shares[2]


def solution(mesh):
    both = ("sub", "slab")
    flat = P(both)
    rows = P(None, both)
    blocks = P(None, None, both)
    placed = (
        rows, P(None, None, None, both), blocks, rows, rows, flat, flat,
        blocks, rows, rows, flat, flat, rows, flat,
    )
    return jax.shard_map(
        on_device, mesh=mesh, in_specs=placed, out_specs=(rows, rows, rows), check_vma=False
    )
```

```python
import jax
import jax.numpy as jnp
from jax import lax
from jax.experimental import pallas as pl
from jax.experimental.pallas import tpu as pltpu
from jax.sharding import PartitionSpec as P

F32 = jnp.float32
BF16 = jnp.bfloat16
MESH = pl.DeviceIdType.MESH

FIRST0, SECOND0, PROLONG0, PROLONG1, FIRST1, SECOND1, FIRST2, OP1, SRC1, OP2, SRC2, CROSS2 = range(12)


def loop(count, body, init=0):
    return lax.fori_loop(0, count, body, init, unroll=True)


LANES = lax.GatherDimensionNumbers(
    offset_dims=(), collapsed_slice_dims=(1,), start_index_map=(1,),
    operand_batching_dims=(0,), start_indices_batching_dims=(0,),
)


def pick_lanes(values, lanes):
    return lax.gather(
        values, lanes[..., None], LANES, slice_sizes=(1, 1), mode=lax.GatherScatterMode.PROMISE_IN_BOUNDS
    )


def lookup(indices, init, base, count, row, flip=0):
    lanes = [(index & 127) ^ flip if flip else index & 127 for index in indices]
    highs = [index >> 7 for index in indices]
    channels = len(init[0])

    held = [list(tile) for tile in init]
    for j in range(count):
        here = [high == base + j for high in highs]
        for c in range(channels):
            spread = jnp.broadcast_to(row(c, j), indices[0].shape)
            for v, lane in enumerate(lanes):
                held[v][c] = jnp.where(here[v], pick_lanes(spread, lane), held[v][c])
    return held


def split(value):
    high = value.astype(BF16)
    return high, (value - high.astype(F32)).astype(BF16)


def against(left, right):
    return lax.dot_general(left, right, (((1,), (1,)), ((), ())), preferred_element_type=F32)


def kernel(
    source_in, operator_in, prolong_in, columns_in, slots_in, aggregates_in, sends_in,
    prolong_one_in, columns_one_in, slots_one_in, aggregates_one_in, sends_one_in,
    columns_two_in, sends_two_in,
    result_ref,
    source_ref, operator_ref, prolong_ref, columns_ref, slots_ref, aggregates_ref, sends_ref,
    prolong_one_ref, columns_one_ref, slots_one_ref, aggregates_one_ref, sends_one_ref,
    columns_two_ref, sends_two_ref,
    turn, index0, slot0, op0, src0, weight0, table0, prolong0, near0, nearp0, blocks0, parts0,
    left0, member0, lifted0, lifted0w, pick_a, pick_b, pick_p, ghost_a, ghost_b, ghost_p,
    op1, src1, index1, slot1, prolong1, table1, near1, nearp1, blocks1, parts1, left1, member1,
    lifted1, lifted1w, x1, send1, pick1_p, pick1_a, pick1_b, ghost1_p, ghost1_a, ghost1_b,
    op2, op2x, src2, src2x, pick2, ghost2, cross2, table_p, terms_p, load_sem, send_sem, recv_sem,
):
    inputs = [
        (sends_in, sends_ref), (prolong_in, prolong_ref), (source_in, source_ref), (operator_in, operator_ref),
        (columns_in, columns_ref), (prolong_one_in, prolong_one_ref), (sends_one_in, sends_one_ref),
        (aggregates_in, aggregates_ref), (slots_in, slots_ref), (columns_one_in, columns_one_ref),
        (slots_one_in, slots_one_ref), (aggregates_one_in, aggregates_one_ref),
        (columns_two_in, columns_two_ref), (sends_two_in, sends_two_ref),
    ]
    loads = {
        id(place): pltpu.make_async_copy(given, place, load_sem.at[i]) for i, (given, place) in enumerate(inputs)
    }
    for _, place in inputs:
        loads[id(place)].start()

    def landed(*places):
        for place in places:
            loads[id(place)].wait()

    sub = lax.axis_index("sub")
    slab = lax.axis_index("slab")
    n_sub = lax.axis_size("sub")
    n_slab = lax.axis_size("slab")
    parity = lax.rem(sub, 2)
    quad = lax.rem(sub // 2, 2)
    has_before = slab > 0
    has_after = slab < n_slab - 1

    barrier = pltpu.get_barrier_semaphore()
    greeted = [(has_before, (sub, slab - 1)), (has_after, (sub, slab + 1))]
    for far in (1, 2, 4):
        greeted += [(sub >= far, (sub - far, slab)), (sub < n_sub - far, (sub + far, slab))]
    across = 2 - 4 * quad
    greeted += [(has_before, (sub + across, slab - 1)), (has_after, (sub + across, slab + 1))]
    greeted += [
        (jnp.logical_and(quad == 0, sub < n_sub - 4), (sub + 6, slab)),
        (jnp.logical_and(quad == 1, sub >= 4), (sub - 6, slab)),
    ]
    for there, peer in greeted:
        @pl.when(there)
        def _(peer=peer):
            pl.semaphore_signal(barrier, inc=1, device_id=peer, device_id_type=MESH)

    def routes(far, shift=0):
        after = (has_after, (sub + shift, slab + 1))
        before = (has_before, (sub + shift, slab - 1))
        upper = (sub < n_sub - far, (sub + far + shift, slab))
        lower = (sub >= far, (sub - far + shift, slab))
        return [(after, before), (before, after), (upper, lower), (lower, upper)]

    def copy(name, d, piece, ghost, peer):
        return pltpu.make_async_remote_copy(
            piece, ghost, send_sem.at[name, d], recv_sem.at[name, d], device_id=peer, device_id_type=MESH
        )

    def part(ghost, d):
        return ghost[d] if isinstance(ghost, list) else ghost.at[d]

    def send(name, far, pieces, ghost, shift=0):
        for d, (to, _) in enumerate(routes(far, shift)):
            @pl.when(to[0])
            def _(d=d, to=to):
                copy(name, d, pieces[d], part(ghost, d), to[1]).start()

    def receive(name, far, pieces, ghost, shift=0):
        for d, (_, source) in enumerate(routes(far, shift)):
            @pl.when(source[0])
            def _(d=d, source=source):
                copy(name, d, pieces[d], part(ghost, d), source[1]).wait_recv()

    def finish(name, far, pieces, ghost, shift=0):
        for d, (to, _) in enumerate(routes(far, shift)):
            @pl.when(to[0])
            def _(d=d, to=to):
                copy(name, d, pieces[d], part(ghost, d), to[1]).wait_send()

    def clear(far, ghosts):
        for d, (_, source) in enumerate(routes(far)):
            @pl.when(jnp.logical_not(source[0]))
            def _(d=d):
                for ghost in ghosts:
                    ghost[d] = jnp.zeros_like(ghost[d])

    clear(1, (ghost_a, ghost_b))
    for d, (_, giver) in enumerate(routes(1)):
        @pl.when(jnp.logical_not(giver[0]))
        def _(d=d):
            ghost_p[64 * d:64 * d + 64] = jnp.zeros((64, 128), F32)
    clear(2, (ghost1_a, ghost1_b, ghost1_p))
    clear(4, (ghost2, cross2))

    zeros = tuple(jnp.zeros((8, 128), F32) for _ in range(4))

    def pick0(row, group, keep):
        got = lookup([sends_ref[0:8, :], sends_ref[8:16, :]], (zeros,) * 2, 0, 16, lambda c, j: row(4 * group + c, j))
        for h in range(2):
            for c in range(4):
                keep(h, 4 * group + c, got[h][c])

    def keep_in(pick):
        def keep(h, c, got):
            pick[2 * h, c] = got[0:4]
            pick[2 * h + 1, c] = got[4:8]

        return keep

    def keep_prolong(h, c, got):
        pick_p[pl.ds(128 * h + c, 8, 16), :] = got

    def table_row(c, j):
        return table0[c, j // 8, pl.ds(j % 8, 1), :]

    def faces0(pick):
        return [pick.at[1], pick.at[0], pick.at[3], pick.at[2]]

    faces_p = [pick_p.at[pl.ds(64 * d, 64), :] for d in (1, 0, 3, 2)]
    ghosts_p = [ghost_p.at[pl.ds(64 * d, 64), :] for d in range(4)]

    landed(sends_ref, prolong_ref)

    def spread_prolong(a, _):
        for h in range(2):
            for b in range(4):
                prolong0[4 * a + b, h] = prolong_ref[a, pl.ds(32 * h + b, 8, 4), :]
        return 0

    lax.fori_loop(0, 4, spread_prolong, 0, unroll=True)

    def pick_prolong(group, _):
        pick0(lambda c, j: prolong0[c, j // 8, pl.ds(j % 8, 1), :], group, keep_prolong)
        return 0

    lax.fori_loop(0, 4, pick_prolong, 0, unroll=True)

    landed(source_ref, operator_ref)
    for h in range(2):
        for a in range(4):
            src0[a, h] = source_ref[pl.ds(32 * h + a, 8, 4), :]

    def weigh(a, _):
        for h in range(2):
            def slot_body(k, total):
                for c in range(4):
                    value = operator_ref[4 * k + a, pl.ds(32 * h + c, 8, 4), :]
                    op0[16 * k + 4 * a + c, h] = value
                    total = total + jnp.abs(value)
                return total

            total = loop(7, slot_body, jnp.ones((8, 128), F32))
            weight0[a, h] = total
            table0[a, h] = src0[a, h] / total
        return 0

    lax.fori_loop(0, 4, weigh, 0, unroll=True)
    pick0(table_row, 0, keep_in(pick_a))

    present = sum(there.astype(jnp.int32) for there, _ in greeted)
    pl.semaphore_wait(barrier, present)

    send(FIRST0, 1, faces0(pick_a), ghost_a)
    send(PROLONG0, 1, faces_p, ghosts_p)

    landed(columns_ref, slots_ref, aggregates_ref)
    for j in range(16):
        turn[8 * j:8 * j + 7] = columns_ref[:, pl.ds(128 * j, 128)]
    for k in range(7):
        for h in range(2):
            index0[2 * k + h] = turn[pl.ds(64 * h + k, 8, 8), :]
    for j in range(16):
        turn[8 * j:8 * j + 7] = slots_ref[:, pl.ds(128 * j, 128)]
    for k in range(7):
        for h in range(2):
            slot0[2 * k + h] = turn[pl.ds(64 * h + k, 8, 8), :]

    def own0(v):
        got = lookup([index0[2 * v], index0[2 * v + 1]], (zeros,) * 2, 0, 16, table_row)
        for q in range(2):
            for c in range(4):
                near0[c, 2 * v + q] = got[q][c]

    def ghost0(ghost, v):
        held = [tuple(near0[c, 2 * v + q] for c in range(4)) for q in range(2)]
        got = lookup(
            [index0[2 * v], index0[2 * v + 1]], held, 16, 16, lambda c, j: ghost[j // 4, c, pl.ds(j % 4, 1), :]
        )
        for q in range(2):
            for c in range(4):
                near0[c, 2 * v + q] = got[q][c]

    def residual0(h):
        totals = []
        for a in range(4):
            def body(k, total):
                for c in range(4):
                    total = total + op0[16 * k + 4 * a + c, h] * near0[c, 2 * k + h]
                return total

            totals.append(src0[a, h] - loop(7, body, jnp.zeros((8, 128), F32)))
        return totals

    def each(count, function, unroll=True):
        def body(i, _):
            function(i)
            return 0

        lax.fori_loop(0, count, body, 0, unroll=unroll)

    each(7, own0)
    receive(FIRST0, 1, faces0(pick_a), ghost_a)
    each(7, lambda v: ghost0(ghost_a, v))
    for h in range(2):
        rest = residual0(h)
        for a in range(4):
            value = table0[a, h] + rest[a] / weight0[a, h]
            table0[a, h] = value
            result_ref[pl.ds(32 * h + a, 8, 4), :] = value
    pick0(table_row, 0, keep_in(pick_b))
    send(SECOND0, 1, faces0(pick_b), ghost_b)

    for j in range(16):
        rows = lax.broadcasted_iota(jnp.int32, (256, 128), 0)
        member0[:, pl.ds(128 * j, 128)] = jnp.where(
            rows == aggregates_ref[j:j + 1, :], 1.0, 0.0
        ).astype(BF16)
    for j in range(16):
        rows = pl.ds(16 * (j // 2), 16)
        for c in range(4):
            table_p[pl.ds(16 * (j // 2) + 4 * c, 4), pl.ds(128 * (j % 2), 128)] = prolong_ref[c, 4 * j:4 * j + 4, :]
    receive(PROLONG0, 1, faces_p, ghosts_p)
    for j in range(16):
        rows = pl.ds(128 + 16 * (j // 2), 16)
        table_p[rows, pl.ds(128 * (j % 2), 128)] = ghost_p[16 * j:16 * j + 16]
    high, low = split(table_p[...])
    terms_p[0:256] = high
    terms_p[256:512] = low

    def blocks_near(k):
        own0(k)
        index = columns_ref[pl.ds(k, 1), :]
        within = index & 255
        group = index >> 8
        rows = lax.broadcasted_iota(jnp.int32, (256, 2048), 0)
        chosen = jnp.where(rows == within, 1.0, 0.0).astype(BF16)
        both = jnp.dot(terms_p[...], chosen, preferred_element_type=F32)
        found = jnp.zeros((16, 2048), F32)
        for g in range(16):
            found = jnp.where(group == g, both[16 * g:16 * g + 16] + both[256 + 16 * g:272 + 16 * g], found)
        for j in range(16):
            nearp0[pl.ds(pl.multiple_of(256 * k + 16 * j, 8), 16), :] = found[:, 128 * j:128 * j + 128]

    each(7, blocks_near)

    def product0(v):
        k, h = v >> 1, v & 1
        for d in range(4):
            near = [nearp0[pl.ds(128 * v + 4 * c + d, 8, 16), :] for c in range(4)]
            inner = []
            for a in range(4):
                total = op0[16 * k + 4 * a, h] * near[0]
                for c in range(1, 4):
                    total = total + op0[16 * k + 4 * a + c, h] * near[c]
                inner.append(total)
            for b in range(4):
                total = prolong0[b, h] * inner[0]
                for a in range(1, 4):
                    total = total + prolong0[4 * a + b, h] * inner[a]
                blocks0[v, 4 * b + d] = total

    each(14, product0)

    def gather_slots0(bd):
        for h in range(2):
            gather_half0(bd, h)

    def gather_half0(bd, h):
        blocks = [blocks0[2 * k + h, bd] for k in range(7)]
        slots = [slot0[2 * k + h] for k in range(7)]
        for s in range(7):
            total = jnp.zeros((8, 128), F32)
            for k in range(7):
                total = total + jnp.where(slots[k] == s, blocks[k], 0.0)
            parts0[pl.ds(pl.multiple_of(256 * s + 16 * bd + 8 * h, 8), 8), :] = total

    each(16, gather_slots0, 4)
    for j in range(16):
        high, low = split(parts0[pl.ds(j, 112, 16), :])
        left0[0:112, pl.ds(128 * j, 128)] = high
        left0[112:224, pl.ds(128 * j, 128)] = low
    both = against(left0[...], member0[...])
    coarse = both[0:112] + both[112:224]
    half = pl.multiple_of(224 * parity, 8)
    for jj in range(2):
        op1[pl.ds(half + 112 * jj, 112), :] = coarse[:, 128 * jj:128 * jj + 128]

    partner = (sub + 1 - 2 * parity, slab)
    mate = (sub + 2 - 4 * quad, slab)
    op1_half = op1.at[pl.ds(half, 224), :]
    op1_other = op1.at[pl.ds(pl.multiple_of(224 - 224 * parity, 8), 224), :]
    copy(OP1, 0, op1_half, op1_half, partner).start()

    receive(SECOND0, 1, faces0(pick_b), ghost_b)
    each(7, lambda v: ghost0(ghost_b, v))
    for h in range(2):
        rest = residual0(h)
        for b in range(4):
            total = prolong0[b, h] * rest[0]
            for a in range(1, 4):
                total = total + prolong0[4 * a + b, h] * rest[a]
            lifted0[pl.ds(32 * h + b, 8, 4), :] = total
    for j in range(16):
        value = lifted0[4 * j:4 * j + 4]
        lifted0w[0:4, pl.ds(128 * j, 128)] = value
        lifted0w[4:8, pl.ds(128 * j, 128)] = value - value.astype(BF16).astype(F32)
    both = against(lifted0w[...].astype(BF16), member0[...])
    coarse = both[0:4] + both[4:8]
    for jj in range(2):
        src1[2 * parity + jj] = coarse[:, 128 * jj:128 * jj + 128]
    src1_half = src1.at[pl.ds(2 * parity, 2)]
    src1_other = src1.at[pl.ds(2 - 2 * parity, 2)]
    copy(SRC1, 0, src1_half, src1_half, partner).start()

    landed(prolong_one_ref, columns_one_ref, slots_one_ref, sends_one_ref)
    for g in range(4):
        for a in range(4):
            prolong1[pl.ds(16 * a + g, 4, 4), :] = prolong_one_ref[a, :, pl.ds(128 * g, 128)]
        index1[pl.ds(g, 7, 4), :] = columns_one_ref[:, pl.ds(128 * g, 128)]
        slot1[pl.ds(g, 7, 4), :] = slots_one_ref[:, pl.ds(128 * g, 128)]
    index1[28:32] = jnp.zeros((4, 128), jnp.int32)
    send1[...] = jnp.zeros((8, 128), jnp.int32)
    send1[0:3] = sends_one_ref[...]

    def pick1(table, pick, group):
        index = send1[...]
        [got] = lookup([index], [zeros], 0, 4, lambda c, j: table[pl.ds(4 * (4 * group + c) + j, 1), :])
        for c in range(4):
            for r in range(3):
                pick[r, pl.ds(4 * group + c, 1), :] = got[c][r:r + 1]

    def faces1(pick):
        return [pick.at[1], pick.at[0], pick.at[2], pick.at[2]]

    for group in range(4):
        pick1(prolong1, pick1_p, group)
    send(PROLONG1, 2, faces1(pick1_p), ghost1_p)

    def tiles1(pair):
        return [index1[16 * pair + 8 * v:16 * pair + 8 * v + 8] for v in range(2)]

    def own1(table, near, group):
        for pair in range(2):
            got = lookup(tiles1(pair), (zeros,) * 2, 0, 4, lambda c, j: table[pl.ds(4 * (4 * group + c) + j, 1), :])
            for v in range(2):
                for c in range(4):
                    near[4 * group + c, 16 * pair + 8 * v:16 * pair + 8 * v + 8, :] = got[v][c]

    upper_lanes = lax.broadcasted_iota(jnp.int32, (1, 128), 1) >= 64

    def ghost1(ghost, near, group):
        def last(c, j):
            channel = pl.ds(4 * group + c, 1)
            return jnp.where(upper_lanes, ghost[2, channel, :], ghost[3, channel, :])

        for pair in range(2):
            places = [pl.ds(16 * pair + 8 * v, 8) for v in range(2)]
            got = [tuple(near[4 * group + c, place, :] for c in range(4)) for place in places]
            got = lookup(tiles1(pair), got, 4, 2, lambda c, j: ghost[j, pl.ds(4 * group + c, 1), :])
            got = lookup(tiles1(pair), got, 6, 1, last, flip=64)
            for v in range(2):
                for c in range(4):
                    near[4 * group + c, places[v], :] = got[v][c]

    copy(OP1, 0, op1_half, op1_other, partner).wait_recv()

    def block1(k, a, c):
        return op1[pl.ds(16 * k + 4 * a + c, 4, 112), :]

    weight1 = []
    for a in range(4):
        def body(k, total):
            for c in range(4):
                total = total + jnp.abs(block1(k, a, c))
            return total

        weight1.append(loop(7, body, jnp.ones((4, 128), F32)))

    copy(SRC1, 0, src1_half, src1_other, partner).wait_recv()

    source1 = []
    first1 = []
    for a in range(4):
        source1.append(jnp.concatenate([src1[g, a:a + 1, :] for g in range(4)], axis=0))
        first1.append(source1[a] / weight1[a])
        table1[4 * a:4 * a + 4] = first1[a]
    pick1(table1, pick1_a, 0)
    send(FIRST1, 2, faces1(pick1_a), ghost1_a)
    own1(table1, near1, 0)

    each(4, lambda i: own1(prolong1, nearp1, i), False)
    receive(PROLONG1, 2, faces1(pick1_p), ghost1_p)
    each(4, lambda i: ghost1(ghost1_p, nearp1, i), False)
    landed(aggregates_one_ref, columns_two_ref, sends_two_ref)
    for g in range(4):
        rows = lax.broadcasted_iota(jnp.int32, (128, 128), 0)
        member1[:, pl.ds(128 * g, 128)] = jnp.where(
            rows == aggregates_one_ref[g:g + 1, :] + 64 * quad, 1.0, 0.0
        ).astype(BF16)

    def product1(k):
        for d in range(4):
            near = [nearp1[4 * c + d, pl.ds(4 * k, 4), :] for c in range(4)]
            inner = []
            for a in range(4):
                total = block1(k, a, 0) * near[0]
                for c in range(1, 4):
                    total = total + block1(k, a, c) * near[c]
                inner.append(total)
            for b in range(4):
                total = prolong1[4 * b:4 * b + 4] * inner[0]
                for a in range(1, 4):
                    total = total + prolong1[16 * a + 4 * b:16 * a + 4 * b + 4] * inner[a]
                blocks1[k, 4 * b + d] = total

    each(7, product1)

    def gather_slots1(bd):
        blocks = [blocks1[k, bd] for k in range(7)]
        slots = [slot1[4 * k:4 * k + 4] for k in range(7)]
        for s in range(7):
            total = jnp.zeros((4, 128), F32)
            for k in range(7):
                total = total + jnp.where(slots[k] == s, blocks[k], 0.0)
            parts1[16 * s + bd] = total

    each(16, gather_slots1)
    for g in range(4):
        high, low = split(parts1[:, g, :])
        left1[0:112, pl.ds(128 * g, 128)] = high
        left1[112:224, pl.ds(128 * g, 128)] = low
    both = against(left1[...], member1[...])
    op2[...] = both[0:112] + both[112:224]
    copy(OP2, 0, op2, op2x, mate).start()

    def residual1():
        totals = []
        for a in range(4):
            def body(k, total):
                for c in range(4):
                    total = total + block1(k, a, c) * near1[c, pl.ds(4 * k, 4), :]
                return total

            totals.append(source1[a] - loop(7, body, jnp.zeros((4, 128), F32)))
        return totals

    receive(FIRST1, 2, faces1(pick1_a), ghost1_a)
    ghost1(ghost1_a, near1, 0)
    rest = residual1()
    for a in range(4):
        value = first1[a] + rest[a] / weight1[a]
        table1[4 * a:4 * a + 4] = value
        x1[pl.ds(a, 4, 4), :] = value
    pick1(table1, pick1_b, 0)
    send(SECOND1, 2, faces1(pick1_b), ghost1_b)
    own1(table1, near1, 0)
    for jj in range(2):
        result_ref[64 + 4 * jj:68 + 4 * jj, :] = jnp.where(
            parity == 0, x1[4 * jj:4 * jj + 4], x1[8 + 4 * jj:12 + 4 * jj]
        )
    copy(OP2, 0, op2, op2x, mate).wait_recv()
    copy(OP2, 0, op2, op2x, mate).wait_send()
    op2[...] = op2[...] + op2x[...]
    block2 = [[op2[pl.ds(4 * a + c, 7, 16), :] for c in range(4)] for a in range(4)]
    weight2 = []
    for a in range(4):
        total = jnp.abs(block2[a][0])
        for c in range(1, 4):
            total = total + jnp.abs(block2[a][c])
        weight2.append(1.0 + jnp.sum(total, axis=0, keepdims=True))

    receive(SECOND1, 2, faces1(pick1_b), ghost1_b)
    ghost1(ghost1_b, near1, 0)
    rest = residual1()
    for b in range(4):
        total = prolong1[4 * b:4 * b + 4] * rest[0]
        for a in range(1, 4):
            total = total + prolong1[16 * a + 4 * b:16 * a + 4 * b + 4] * rest[a]
        lifted1[pl.ds(b, 4, 4), :] = total
    for g in range(4):
        value = lifted1[4 * g:4 * g + 4]
        lifted1w[0:4, pl.ds(128 * g, 128)] = value
        lifted1w[4:8, pl.ds(128 * g, 128)] = value - value.astype(BF16).astype(F32)
    both = against(lifted1w[...].astype(BF16), member1[...])
    half2 = both[0:4] + both[4:8]
    src2[0:4] = half2
    for a in range(4):
        src2[4 + a:5 + a] = half2[a:a + 1] / weight2[a]
    copy(SRC2, 0, src2, src2x, mate).start()

    faces_row = jnp.reshape(sends_two_ref[0:128], (1, 128))
    sides_row = jnp.reshape(sends_two_ref[32:160], (1, 128))
    for r, listed in enumerate((faces_row, sides_row)):
        [picks] = lookup(
            [jnp.broadcast_to(listed, (8, 128))], [zeros], 0, 1, lambda c, j: src2[4 + c:5 + c]
        )
        for c in range(4):
            pick2[r, c:c + 1] = picks[c][0:1]
    faces2 = [pick2.at[0], pick2.at[0], pick2.at[1], pick2.at[1]]
    send(FIRST2, 4, faces2, ghost2)
    send(CROSS2, 4, faces2, cross2, across)
    index = columns_two_ref[...]
    lane = lax.broadcasted_iota(jnp.int32, (1, 128), 1)
    wide = tuple(jnp.zeros((7, 128), F32) for _ in range(4))
    copy(SRC2, 0, src2, src2x, mate).wait_recv()
    whole2 = src2[...] + src2x[...]
    source2 = whole2[0:4]
    first2 = [whole2[4 + a:5 + a] for a in range(4)]
    near = lookup([index], [wide], 0, 1, lambda c, j: first2[c])
    receive(FIRST2, 4, faces2, ghost2)
    receive(CROSS2, 4, faces2, cross2, across)

    def ghost_row(d, c):
        return ghost2[d, c:c + 1] + cross2[d, c:c + 1]

    near = lookup(
        [index], near, 1, 1, lambda c, j: jnp.where(lane >= 64, ghost_row(0, c), ghost_row(1, c)), flip=64
    )
    [near] = lookup(
        [index], near, 2, 1, lambda c, j: jnp.where(lane >= 112, ghost_row(2, c), ghost_row(3, c)), flip=112
    )
    place = lax.rem(sub, 4)
    for a in range(4):
        total = block2[a][0] * near[0]
        for c in range(1, 4):
            total = total + block2[a][c] * near[c]
        rest2 = source2[a:a + 1] - jnp.sum(total, axis=0, keepdims=True)
        value = first2[a] + rest2 / weight2[a]
        share = value[:, 0:32]
        for q in range(1, 4):
            share = jnp.where(place == q, value[:, 32 * q:32 * q + 32], share)
        result_ref[72 + a:73 + a, 0:32] = share

    finish(FIRST0, 1, faces0(pick_a), ghost_a)
    finish(PROLONG0, 1, faces_p, ghosts_p)
    finish(PROLONG1, 2, faces1(pick1_p), ghost1_p)
    finish(SECOND0, 1, faces0(pick_b), ghost_b)
    finish(FIRST1, 2, faces1(pick1_a), ghost1_a)
    finish(SECOND1, 2, faces1(pick1_b), ghost1_b)
    finish(FIRST2, 4, faces2, ghost2)
    finish(CROSS2, 4, faces2, cross2, across)
    copy(OP1, 0, op1_half, op1_half, partner).wait_send()
    copy(SRC1, 0, src1_half, src1_half, partner).wait_send()
    copy(SRC2, 0, src2, src2x, mate).wait_send()


def fanout(result_ref, fine_ref, one_ref, two_ref):
    fine_ref[...] = result_ref[0:64]
    one_ref[...] = result_ref[64:72]
    two_ref[...] = result_ref[72:76, 0:32]


def fold(array):
    lead = array.shape[:-2]
    shaped = array.reshape(lead + (array.shape[-2], 16, 128))
    return jnp.swapaxes(shaped, -3, -2).reshape(lead + (16 * array.shape[-2], 128))


def on_device(
    source, operator, prolong, columns, slots, aggregates, sends,
    prolong_one, columns_one, slots_one, aggregates_one, sends_one, columns_two, sends_two,
):
    vmem = pl.BlockSpec(memory_space=pltpu.VMEM)
    landing = [
        ((64, 128), F32), ((28, 64, 128), F32), ((4, 64, 128), F32), ((7, 2048), jnp.int32), ((7, 2048), jnp.int32),
        ((16, 128), jnp.int32), ((16, 128), jnp.int32), ((4, 4, 512), F32), ((7, 512), jnp.int32),
        ((7, 512), jnp.int32), ((4, 128), jnp.int32), ((3, 128), jnp.int32), ((7, 128), jnp.int32),
        ((160,), jnp.int32),
    ]
    scratch = landing + [
        ((128, 128), jnp.int32), ((14, 8, 128), jnp.int32), ((14, 8, 128), jnp.int32),
        ((112, 2, 8, 128), F32), ((4, 2, 8, 128), F32), ((4, 2, 8, 128), F32), ((4, 2, 8, 128), F32),
        ((16, 2, 8, 128), F32), ((4, 14, 8, 128), F32), ((1792, 128), F32),
        ((14, 16, 8, 128), F32), ((1792, 128), F32), ((224, 2048), BF16), ((256, 2048), BF16),
        ((64, 128), F32), ((8, 2048), F32),
        ((4, 4, 4, 128), F32), ((4, 4, 4, 128), F32), ((256, 128), F32),
        ((4, 4, 4, 128), F32), ((4, 4, 4, 128), F32), ((256, 128), F32),
        ((448, 128), F32), ((4, 4, 128), F32), ((32, 128), jnp.int32), ((32, 128), jnp.int32),
        ((64, 128), F32), ((16, 128), F32), ((4, 32, 128), F32), ((16, 32, 128), F32),
        ((7, 16, 4, 128), F32), ((112, 4, 128), F32), ((224, 512), BF16), ((128, 512), BF16),
        ((16, 128), F32), ((8, 512), F32), ((16, 128), F32), ((8, 128), jnp.int32),
        ((3, 16, 128), F32), ((3, 4, 128), F32), ((3, 4, 128), F32),
        ((4, 16, 128), F32), ((4, 4, 128), F32), ((4, 4, 128), F32),
        ((112, 128), F32), ((112, 128), F32), ((8, 128), F32), ((8, 128), F32),
        ((2, 4, 128), F32), ((4, 4, 128), F32), ((4, 4, 128), F32), ((256, 256), F32), ((512, 256), BF16),
    ]
    result = pl.pallas_call(
        kernel,
        out_shape=jax.ShapeDtypeStruct((80, 128), F32),
        in_specs=[pl.BlockSpec(memory_space=pl.ANY)] * 14,
        out_specs=vmem,
        scratch_shapes=[pltpu.VMEM(shape, kind) for shape, kind in scratch]
        + [pltpu.SemaphoreType.DMA(shape) for shape in ((14,), (12, 4), (12, 4))],
        compiler_params=pltpu.CompilerParams(
            collective_id=0, has_side_effects=True, vmem_limit_bytes=60 << 20
        ),
        name="descend",
    )(
        fold(source), fold(operator).reshape(28, 64, 128), fold(prolong), columns, slots,
        aggregates.reshape(16, 128), sends.reshape(16, 128),
        prolong_one, columns_one, slots_one, aggregates_one.reshape(4, 128), sends_one.reshape(3, 128),
        columns_two, sends_two,
    )
    shares = pl.pallas_call(
        fanout,
        out_shape=[jax.ShapeDtypeStruct(shape, F32) for shape in ((64, 128), (8, 128), (4, 32))],
        in_specs=[vmem],
        out_specs=[vmem] * 3,
        name="fanout",
    )(result)

    def unfold(rows):
        return rows.reshape(-1, 4, 128).swapaxes(0, 1).reshape(4, -1)

    return unfold(shares[0]), unfold(shares[1]), shares[2]


def solution(mesh):
    both = ("sub", "slab")
    flat = P(both)
    rows = P(None, both)
    blocks = P(None, None, both)
    placed = (
        rows, P(None, None, None, both), blocks, rows, rows, flat, flat,
        blocks, rows, rows, flat, flat, rows, flat,
    )
    return jax.shard_map(
        on_device, mesh=mesh, in_specs=placed, out_specs=(rows, rows, rows), check_vma=False
    )
```

```python
import jax
import jax.numpy as jnp
from jax import lax
from jax.experimental import pallas as pl
from jax.experimental.pallas import tpu as pltpu
from jax.sharding import PartitionSpec as P

F32 = jnp.float32
BF16 = jnp.bfloat16
MESH = pl.DeviceIdType.MESH

FIRST0, SECOND0, PROLONG0, PROLONG1, FIRST1, SECOND1, FIRST2, OP1, SRC1, OP2, SRC2, CROSS2 = range(12)


def loop(count, body, init=0):
    return lax.fori_loop(0, count, body, init, unroll=True)


LANES = lax.GatherDimensionNumbers(
    offset_dims=(), collapsed_slice_dims=(1,), start_index_map=(1,),
    operand_batching_dims=(0,), start_indices_batching_dims=(0,),
)


def pick_lanes(values, lanes):
    return lax.gather(
        values, lanes[..., None], LANES, slice_sizes=(1, 1), mode=lax.GatherScatterMode.PROMISE_IN_BOUNDS
    )


def lookup(indices, init, base, count, row, flip=0):
    lanes = [(index & 127) ^ flip if flip else index & 127 for index in indices]
    highs = [index >> 7 for index in indices]
    channels = len(init[0])

    held = [list(tile) for tile in init]
    for j in range(count):
        here = [high == base + j for high in highs]
        for c in range(channels):
            spread = jnp.broadcast_to(row(c, j), indices[0].shape)
            for v, lane in enumerate(lanes):
                held[v][c] = jnp.where(here[v], pick_lanes(spread, lane), held[v][c])
    return held


def split(value):
    high = value.astype(BF16)
    return high, (value - high.astype(F32)).astype(BF16)


def against(left, right):
    return lax.dot_general(left, right, (((1,), (1,)), ((), ())), preferred_element_type=F32)


def kernel(
    source_in, operator_in, prolong_in, columns_in, slots_in, aggregates_in, sends_in,
    prolong_one_in, columns_one_in, slots_one_in, aggregates_one_in, sends_one_in,
    columns_two_in, sends_two_in,
    result_ref,
    source_ref, operator_ref, prolong_ref, columns_ref, slots_ref, aggregates_ref, sends_ref,
    prolong_one_ref, columns_one_ref, slots_one_ref, aggregates_one_ref, sends_one_ref,
    columns_two_ref, sends_two_ref,
    turn, index0, slot0, op0, src0, weight0, table0, prolong0, near0, nearp0, blocks0, parts0,
    left0, member0, lifted0, lifted0w, pick_a, pick_b, pick_p, ghost_a, ghost_b, ghost_p,
    op1, src1, index1, slot1, prolong1, table1, near1, nearp1, blocks1, parts1, left1, member1,
    lifted1, lifted1w, x1, send1, pick1_p, pick1_a, pick1_b, ghost1_p, ghost1_a, ghost1_b,
    op2, op2x, src2, src2x, pick2, ghost2, cross2, table_p, terms_p, load_sem, send_sem, recv_sem,
):
    inputs = [
        (sends_in, sends_ref), (prolong_in, prolong_ref), (source_in, source_ref), (operator_in, operator_ref),
        (columns_in, columns_ref), (prolong_one_in, prolong_one_ref), (sends_one_in, sends_one_ref),
        (aggregates_in, aggregates_ref), (slots_in, slots_ref), (columns_one_in, columns_one_ref),
        (slots_one_in, slots_one_ref), (aggregates_one_in, aggregates_one_ref),
        (columns_two_in, columns_two_ref), (sends_two_in, sends_two_ref),
    ]
    loads = {
        id(place): pltpu.make_async_copy(given, place, load_sem.at[i]) for i, (given, place) in enumerate(inputs)
    }
    for _, place in inputs:
        loads[id(place)].start()

    def landed(*places):
        for place in places:
            loads[id(place)].wait()

    sub = lax.axis_index("sub")
    slab = lax.axis_index("slab")
    n_sub = lax.axis_size("sub")
    n_slab = lax.axis_size("slab")
    parity = lax.rem(sub, 2)
    quad = lax.rem(sub // 2, 2)
    has_before = slab > 0
    has_after = slab < n_slab - 1

    barrier = pltpu.get_barrier_semaphore()
    greeted = [(has_before, (sub, slab - 1)), (has_after, (sub, slab + 1))]
    for far in (1, 2, 4):
        greeted += [(sub >= far, (sub - far, slab)), (sub < n_sub - far, (sub + far, slab))]
    across = 2 - 4 * quad
    greeted += [(has_before, (sub + across, slab - 1)), (has_after, (sub + across, slab + 1))]
    greeted += [
        (jnp.logical_and(quad == 0, sub < n_sub - 4), (sub + 6, slab)),
        (jnp.logical_and(quad == 1, sub >= 4), (sub - 6, slab)),
    ]
    for there, peer in greeted:
        @pl.when(there)
        def _(peer=peer):
            pl.semaphore_signal(barrier, inc=1, device_id=peer, device_id_type=MESH)

    def routes(far, shift=0):
        after = (has_after, (sub + shift, slab + 1))
        before = (has_before, (sub + shift, slab - 1))
        upper = (sub < n_sub - far, (sub + far + shift, slab))
        lower = (sub >= far, (sub - far + shift, slab))
        return [(after, before), (before, after), (upper, lower), (lower, upper)]

    def copy(name, d, piece, ghost, peer):
        return pltpu.make_async_remote_copy(
            piece, ghost, send_sem.at[name, d], recv_sem.at[name, d], device_id=peer, device_id_type=MESH
        )

    def part(ghost, d):
        return ghost[d] if isinstance(ghost, list) else ghost.at[d]

    def send(name, far, pieces, ghost, shift=0):
        for d, (to, _) in enumerate(routes(far, shift)):
            @pl.when(to[0])
            def _(d=d, to=to):
                copy(name, d, pieces[d], part(ghost, d), to[1]).start()

    def receive(name, far, pieces, ghost, shift=0):
        for d, (_, source) in enumerate(routes(far, shift)):
            @pl.when(source[0])
            def _(d=d, source=source):
                copy(name, d, pieces[d], part(ghost, d), source[1]).wait_recv()

    def finish(name, far, pieces, ghost, shift=0):
        for d, (to, _) in enumerate(routes(far, shift)):
            @pl.when(to[0])
            def _(d=d, to=to):
                copy(name, d, pieces[d], part(ghost, d), to[1]).wait_send()

    def clear(far, ghosts):
        for d, (_, source) in enumerate(routes(far)):
            @pl.when(jnp.logical_not(source[0]))
            def _(d=d):
                for ghost in ghosts:
                    ghost[d] = jnp.zeros_like(ghost[d])

    clear(1, (ghost_a, ghost_b))
    for d, (_, giver) in enumerate(routes(1)):
        @pl.when(jnp.logical_not(giver[0]))
        def _(d=d):
            ghost_p[64 * d:64 * d + 64] = jnp.zeros((64, 128), F32)
    clear(2, (ghost1_a, ghost1_b, ghost1_p))
    clear(4, (ghost2, cross2))

    zeros = tuple(jnp.zeros((8, 128), F32) for _ in range(4))

    def pick0(row, group, keep):
        got = lookup([sends_ref[0:8, :], sends_ref[8:16, :]], (zeros,) * 2, 0, 16, lambda c, j: row(4 * group + c, j))
        for h in range(2):
            for c in range(4):
                keep(h, 4 * group + c, got[h][c])

    def keep_in(pick):
        def keep(h, c, got):
            pick[2 * h, c] = got[0:4]
            pick[2 * h + 1, c] = got[4:8]

        return keep

    def keep_prolong(h, c, got):
        pick_p[pl.ds(128 * h + c, 8, 16), :] = got

    def table_row(c, j):
        return table0[c, j // 8, pl.ds(j % 8, 1), :]

    def faces0(pick):
        return [pick.at[1], pick.at[0], pick.at[3], pick.at[2]]

    faces_p = [pick_p.at[pl.ds(64 * d, 64), :] for d in (1, 0, 3, 2)]
    ghosts_p = [ghost_p.at[pl.ds(64 * d, 64), :] for d in range(4)]

    landed(sends_ref, prolong_ref)

    def spread_prolong(a, _):
        for h in range(2):
            for b in range(4):
                prolong0[4 * a + b, h] = prolong_ref[a, pl.ds(32 * h + b, 8, 4), :]
        return 0

    lax.fori_loop(0, 4, spread_prolong, 0, unroll=True)

    def pick_prolong(group, _):
        pick0(lambda c, j: prolong0[c, j // 8, pl.ds(j % 8, 1), :], group, keep_prolong)
        return 0

    lax.fori_loop(0, 4, pick_prolong, 0, unroll=True)

    landed(source_ref, operator_ref)
    for h in range(2):
        for a in range(4):
            src0[a, h] = source_ref[pl.ds(32 * h + a, 8, 4), :]

    def weigh(a, _):
        for h in range(2):
            def slot_body(k, total):
                for c in range(4):
                    value = operator_ref[4 * k + a, pl.ds(32 * h + c, 8, 4), :]
                    op0[16 * k + 4 * a + c, h] = value
                    total = total + jnp.abs(value)
                return total

            total = loop(7, slot_body, jnp.ones((8, 128), F32))
            weight0[a, h] = total
            table0[a, h] = src0[a, h] / total
        return 0

    lax.fori_loop(0, 4, weigh, 0, unroll=True)
    pick0(table_row, 0, keep_in(pick_a))

    present = sum(there.astype(jnp.int32) for there, _ in greeted)
    pl.semaphore_wait(barrier, present)

    send(FIRST0, 1, faces0(pick_a), ghost_a)
    send(PROLONG0, 1, faces_p, ghosts_p)

    landed(prolong_one_ref, columns_one_ref, slots_one_ref, sends_one_ref)
    for g in range(4):
        for a in range(4):
            prolong1[pl.ds(16 * a + g, 4, 4), :] = prolong_one_ref[a, :, pl.ds(128 * g, 128)]
        index1[pl.ds(g, 7, 4), :] = columns_one_ref[:, pl.ds(128 * g, 128)]
        slot1[pl.ds(g, 7, 4), :] = slots_one_ref[:, pl.ds(128 * g, 128)]
    index1[28:32] = jnp.zeros((4, 128), jnp.int32)
    send1[...] = jnp.zeros((8, 128), jnp.int32)
    send1[0:3] = sends_one_ref[...]

    def pick1(table, pick, group):
        index = send1[...]
        [got] = lookup([index], [zeros], 0, 4, lambda c, j: table[pl.ds(4 * (4 * group + c) + j, 1), :])
        for c in range(4):
            for r in range(3):
                pick[r, pl.ds(4 * group + c, 1), :] = got[c][r:r + 1]

    def faces1(pick):
        return [pick.at[1], pick.at[0], pick.at[2], pick.at[2]]

    for group in range(4):
        pick1(prolong1, pick1_p, group)
    send(PROLONG1, 2, faces1(pick1_p), ghost1_p)

    landed(columns_ref, slots_ref, aggregates_ref)
    for j in range(16):
        turn[8 * j:8 * j + 7] = columns_ref[:, pl.ds(128 * j, 128)]
    for k in range(7):
        for h in range(2):
            index0[2 * k + h] = turn[pl.ds(64 * h + k, 8, 8), :]
    for j in range(16):
        turn[8 * j:8 * j + 7] = slots_ref[:, pl.ds(128 * j, 128)]
    for k in range(7):
        for h in range(2):
            slot0[2 * k + h] = turn[pl.ds(64 * h + k, 8, 8), :]

    def own0(v):
        got = lookup([index0[2 * v], index0[2 * v + 1]], (zeros,) * 2, 0, 16, table_row)
        for q in range(2):
            for c in range(4):
                near0[c, 2 * v + q] = got[q][c]

    def ghost0(ghost, v):
        held = [tuple(near0[c, 2 * v + q] for c in range(4)) for q in range(2)]
        got = lookup(
            [index0[2 * v], index0[2 * v + 1]], held, 16, 16, lambda c, j: ghost[j // 4, c, pl.ds(j % 4, 1), :]
        )
        for q in range(2):
            for c in range(4):
                near0[c, 2 * v + q] = got[q][c]

    def residual0(h):
        totals = []
        for a in range(4):
            def body(k, total):
                for c in range(4):
                    total = total + op0[16 * k + 4 * a + c, h] * near0[c, 2 * k + h]
                return total

            totals.append(src0[a, h] - loop(7, body, jnp.zeros((8, 128), F32)))
        return totals

    def each(count, function, unroll=True):
        def body(i, _):
            function(i)
            return 0

        lax.fori_loop(0, count, body, 0, unroll=unroll)

    each(7, own0)
    receive(FIRST0, 1, faces0(pick_a), ghost_a)
    each(7, lambda v: ghost0(ghost_a, v))
    for h in range(2):
        rest = residual0(h)
        for a in range(4):
            value = table0[a, h] + rest[a] / weight0[a, h]
            table0[a, h] = value
            result_ref[pl.ds(32 * h + a, 8, 4), :] = value
    pick0(table_row, 0, keep_in(pick_b))
    send(SECOND0, 1, faces0(pick_b), ghost_b)

    for j in range(16):
        rows = lax.broadcasted_iota(jnp.int32, (256, 128), 0)
        member0[:, pl.ds(128 * j, 128)] = jnp.where(
            rows == aggregates_ref[j:j + 1, :], 1.0, 0.0
        ).astype(BF16)
    for j in range(16):
        rows = pl.ds(16 * (j // 2), 16)
        for c in range(4):
            table_p[pl.ds(16 * (j // 2) + 4 * c, 4), pl.ds(128 * (j % 2), 128)] = prolong_ref[c, 4 * j:4 * j + 4, :]
    receive(PROLONG0, 1, faces_p, ghosts_p)
    for j in range(16):
        rows = pl.ds(128 + 16 * (j // 2), 16)
        table_p[rows, pl.ds(128 * (j % 2), 128)] = ghost_p[16 * j:16 * j + 16]
    high, low = split(table_p[...])
    terms_p[0:256] = high
    terms_p[256:512] = low

    def blocks_near(k):
        own0(k)
        index = columns_ref[pl.ds(k, 1), :]
        within = index & 255
        group = index >> 8
        rows = lax.broadcasted_iota(jnp.int32, (256, 2048), 0)
        chosen = jnp.where(rows == within, 1.0, 0.0).astype(BF16)
        both = jnp.dot(terms_p[...], chosen, preferred_element_type=F32)
        found = jnp.zeros((16, 2048), F32)
        for g in range(16):
            found = jnp.where(group == g, both[16 * g:16 * g + 16] + both[256 + 16 * g:272 + 16 * g], found)
        for j in range(16):
            nearp0[pl.ds(pl.multiple_of(256 * k + 16 * j, 8), 16), :] = found[:, 128 * j:128 * j + 128]

    each(7, blocks_near)

    def product0(v):
        k, h = v >> 1, v & 1
        for d in range(4):
            near = [nearp0[pl.ds(128 * v + 4 * c + d, 8, 16), :] for c in range(4)]
            inner = []
            for a in range(4):
                total = op0[16 * k + 4 * a, h] * near[0]
                for c in range(1, 4):
                    total = total + op0[16 * k + 4 * a + c, h] * near[c]
                inner.append(total)
            for b in range(4):
                total = prolong0[b, h] * inner[0]
                for a in range(1, 4):
                    total = total + prolong0[4 * a + b, h] * inner[a]
                blocks0[v, 4 * b + d] = total

    each(14, product0)

    def gather_slots0(bd):
        for h in range(2):
            gather_half0(bd, h)

    def gather_half0(bd, h):
        blocks = [blocks0[2 * k + h, bd] for k in range(7)]
        slots = [slot0[2 * k + h] for k in range(7)]
        for s in range(7):
            total = jnp.zeros((8, 128), F32)
            for k in range(7):
                total = total + jnp.where(slots[k] == s, blocks[k], 0.0)
            parts0[pl.ds(pl.multiple_of(256 * s + 16 * bd + 8 * h, 8), 8), :] = total

    each(16, gather_slots0, 4)
    for j in range(16):
        high, low = split(parts0[pl.ds(j, 112, 16), :])
        left0[0:112, pl.ds(128 * j, 128)] = high
        left0[112:224, pl.ds(128 * j, 128)] = low
    both = against(left0[...], member0[...])
    coarse = both[0:112] + both[112:224]
    half = pl.multiple_of(224 * parity, 8)
    for jj in range(2):
        op1[pl.ds(half + 112 * jj, 112), :] = coarse[:, 128 * jj:128 * jj + 128]

    partner = (sub + 1 - 2 * parity, slab)
    mate = (sub + 2 - 4 * quad, slab)
    op1_half = op1.at[pl.ds(half, 224), :]
    op1_other = op1.at[pl.ds(pl.multiple_of(224 - 224 * parity, 8), 224), :]
    copy(OP1, 0, op1_half, op1_half, partner).start()

    receive(SECOND0, 1, faces0(pick_b), ghost_b)
    each(7, lambda v: ghost0(ghost_b, v))
    for h in range(2):
        rest = residual0(h)
        for b in range(4):
            total = prolong0[b, h] * rest[0]
            for a in range(1, 4):
                total = total + prolong0[4 * a + b, h] * rest[a]
            lifted0[pl.ds(32 * h + b, 8, 4), :] = total
    for j in range(16):
        value = lifted0[4 * j:4 * j + 4]
        lifted0w[0:4, pl.ds(128 * j, 128)] = value
        lifted0w[4:8, pl.ds(128 * j, 128)] = value - value.astype(BF16).astype(F32)
    both = against(lifted0w[...].astype(BF16), member0[...])
    coarse = both[0:4] + both[4:8]
    for jj in range(2):
        src1[2 * parity + jj] = coarse[:, 128 * jj:128 * jj + 128]
    src1_half = src1.at[pl.ds(2 * parity, 2)]
    src1_other = src1.at[pl.ds(2 - 2 * parity, 2)]
    copy(SRC1, 0, src1_half, src1_half, partner).start()

    def tiles1(pair):
        return [index1[16 * pair + 8 * v:16 * pair + 8 * v + 8] for v in range(2)]

    def own1(table, near, group):
        for pair in range(2):
            got = lookup(tiles1(pair), (zeros,) * 2, 0, 4, lambda c, j: table[pl.ds(4 * (4 * group + c) + j, 1), :])
            for v in range(2):
                for c in range(4):
                    near[4 * group + c, 16 * pair + 8 * v:16 * pair + 8 * v + 8, :] = got[v][c]

    upper_lanes = lax.broadcasted_iota(jnp.int32, (1, 128), 1) >= 64

    def ghost1(ghost, near, group):
        def last(c, j):
            channel = pl.ds(4 * group + c, 1)
            return jnp.where(upper_lanes, ghost[2, channel, :], ghost[3, channel, :])

        for pair in range(2):
            places = [pl.ds(16 * pair + 8 * v, 8) for v in range(2)]
            got = [tuple(near[4 * group + c, place, :] for c in range(4)) for place in places]
            got = lookup(tiles1(pair), got, 4, 2, lambda c, j: ghost[j, pl.ds(4 * group + c, 1), :])
            got = lookup(tiles1(pair), got, 6, 1, last, flip=64)
            for v in range(2):
                for c in range(4):
                    near[4 * group + c, places[v], :] = got[v][c]

    copy(OP1, 0, op1_half, op1_other, partner).wait_recv()

    def block1(k, a, c):
        return op1[pl.ds(16 * k + 4 * a + c, 4, 112), :]

    weight1 = []
    for a in range(4):
        def body(k, total):
            for c in range(4):
                total = total + jnp.abs(block1(k, a, c))
            return total

        weight1.append(loop(7, body, jnp.ones((4, 128), F32)))

    copy(SRC1, 0, src1_half, src1_other, partner).wait_recv()

    source1 = []
    first1 = []
    for a in range(4):
        source1.append(jnp.concatenate([src1[g, a:a + 1, :] for g in range(4)], axis=0))
        first1.append(source1[a] / weight1[a])
        table1[4 * a:4 * a + 4] = first1[a]
    pick1(table1, pick1_a, 0)
    send(FIRST1, 2, faces1(pick1_a), ghost1_a)
    own1(table1, near1, 0)

    each(4, lambda i: own1(prolong1, nearp1, i), False)
    receive(PROLONG1, 2, faces1(pick1_p), ghost1_p)
    each(4, lambda i: ghost1(ghost1_p, nearp1, i), False)
    landed(aggregates_one_ref, columns_two_ref, sends_two_ref)
    for g in range(4):
        rows = lax.broadcasted_iota(jnp.int32, (128, 128), 0)
        member1[:, pl.ds(128 * g, 128)] = jnp.where(
            rows == aggregates_one_ref[g:g + 1, :] + 64 * quad, 1.0, 0.0
        ).astype(BF16)

    def product1(k):
        for d in range(4):
            near = [nearp1[4 * c + d, pl.ds(4 * k, 4), :] for c in range(4)]
            inner = []
            for a in range(4):
                total = block1(k, a, 0) * near[0]
                for c in range(1, 4):
                    total = total + block1(k, a, c) * near[c]
                inner.append(total)
            for b in range(4):
                total = prolong1[4 * b:4 * b + 4] * inner[0]
                for a in range(1, 4):
                    total = total + prolong1[16 * a + 4 * b:16 * a + 4 * b + 4] * inner[a]
                blocks1[k, 4 * b + d] = total

    each(7, product1)

    def gather_slots1(bd):
        blocks = [blocks1[k, bd] for k in range(7)]
        slots = [slot1[4 * k:4 * k + 4] for k in range(7)]
        for s in range(7):
            total = jnp.zeros((4, 128), F32)
            for k in range(7):
                total = total + jnp.where(slots[k] == s, blocks[k], 0.0)
            parts1[16 * s + bd] = total

    each(16, gather_slots1)
    for g in range(4):
        high, low = split(parts1[:, g, :])
        left1[0:112, pl.ds(128 * g, 128)] = high
        left1[112:224, pl.ds(128 * g, 128)] = low
    both = against(left1[...], member1[...])
    op2[...] = both[0:112] + both[112:224]
    copy(OP2, 0, op2, op2x, mate).start()

    def residual1():
        totals = []
        for a in range(4):
            def body(k, total):
                for c in range(4):
                    total = total + block1(k, a, c) * near1[c, pl.ds(4 * k, 4), :]
                return total

            totals.append(source1[a] - loop(7, body, jnp.zeros((4, 128), F32)))
        return totals

    receive(FIRST1, 2, faces1(pick1_a), ghost1_a)
    ghost1(ghost1_a, near1, 0)
    rest = residual1()
    for a in range(4):
        value = first1[a] + rest[a] / weight1[a]
        table1[4 * a:4 * a + 4] = value
        x1[pl.ds(a, 4, 4), :] = value
    pick1(table1, pick1_b, 0)
    send(SECOND1, 2, faces1(pick1_b), ghost1_b)
    own1(table1, near1, 0)
    for jj in range(2):
        result_ref[64 + 4 * jj:68 + 4 * jj, :] = jnp.where(
            parity == 0, x1[4 * jj:4 * jj + 4], x1[8 + 4 * jj:12 + 4 * jj]
        )
    copy(OP2, 0, op2, op2x, mate).wait_recv()
    copy(OP2, 0, op2, op2x, mate).wait_send()
    op2[...] = op2[...] + op2x[...]
    block2 = [[op2[pl.ds(4 * a + c, 7, 16), :] for c in range(4)] for a in range(4)]
    weight2 = []
    for a in range(4):
        total = jnp.abs(block2[a][0])
        for c in range(1, 4):
            total = total + jnp.abs(block2[a][c])
        weight2.append(1.0 + jnp.sum(total, axis=0, keepdims=True))

    receive(SECOND1, 2, faces1(pick1_b), ghost1_b)
    ghost1(ghost1_b, near1, 0)
    rest = residual1()
    for b in range(4):
        total = prolong1[4 * b:4 * b + 4] * rest[0]
        for a in range(1, 4):
            total = total + prolong1[16 * a + 4 * b:16 * a + 4 * b + 4] * rest[a]
        lifted1[pl.ds(b, 4, 4), :] = total
    for g in range(4):
        value = lifted1[4 * g:4 * g + 4]
        lifted1w[0:4, pl.ds(128 * g, 128)] = value
        lifted1w[4:8, pl.ds(128 * g, 128)] = value - value.astype(BF16).astype(F32)
    both = against(lifted1w[...].astype(BF16), member1[...])
    half2 = both[0:4] + both[4:8]
    src2[0:4] = half2
    for a in range(4):
        src2[4 + a:5 + a] = half2[a:a + 1] / weight2[a]
    copy(SRC2, 0, src2, src2x, mate).start()

    faces_row = jnp.reshape(sends_two_ref[0:128], (1, 128))
    sides_row = jnp.reshape(sends_two_ref[32:160], (1, 128))
    for r, listed in enumerate((faces_row, sides_row)):
        [picks] = lookup(
            [jnp.broadcast_to(listed, (8, 128))], [zeros], 0, 1, lambda c, j: src2[4 + c:5 + c]
        )
        for c in range(4):
            pick2[r, c:c + 1] = picks[c][0:1]
    faces2 = [pick2.at[0], pick2.at[0], pick2.at[1], pick2.at[1]]
    send(FIRST2, 4, faces2, ghost2)
    send(CROSS2, 4, faces2, cross2, across)
    index = columns_two_ref[...]
    lane = lax.broadcasted_iota(jnp.int32, (1, 128), 1)
    wide = tuple(jnp.zeros((7, 128), F32) for _ in range(4))
    copy(SRC2, 0, src2, src2x, mate).wait_recv()
    whole2 = src2[...] + src2x[...]
    source2 = whole2[0:4]
    first2 = [whole2[4 + a:5 + a] for a in range(4)]
    near = lookup([index], [wide], 0, 1, lambda c, j: first2[c])
    receive(FIRST2, 4, faces2, ghost2)
    receive(CROSS2, 4, faces2, cross2, across)

    def ghost_row(d, c):
        return ghost2[d, c:c + 1] + cross2[d, c:c + 1]

    near = lookup(
        [index], near, 1, 1, lambda c, j: jnp.where(lane >= 64, ghost_row(0, c), ghost_row(1, c)), flip=64
    )
    [near] = lookup(
        [index], near, 2, 1, lambda c, j: jnp.where(lane >= 112, ghost_row(2, c), ghost_row(3, c)), flip=112
    )
    place = lax.rem(sub, 4)
    for a in range(4):
        total = block2[a][0] * near[0]
        for c in range(1, 4):
            total = total + block2[a][c] * near[c]
        rest2 = source2[a:a + 1] - jnp.sum(total, axis=0, keepdims=True)
        value = first2[a] + rest2 / weight2[a]
        share = value[:, 0:32]
        for q in range(1, 4):
            share = jnp.where(place == q, value[:, 32 * q:32 * q + 32], share)
        result_ref[72 + a:73 + a, 0:32] = share

    finish(FIRST0, 1, faces0(pick_a), ghost_a)
    finish(PROLONG0, 1, faces_p, ghosts_p)
    finish(PROLONG1, 2, faces1(pick1_p), ghost1_p)
    finish(SECOND0, 1, faces0(pick_b), ghost_b)
    finish(FIRST1, 2, faces1(pick1_a), ghost1_a)
    finish(SECOND1, 2, faces1(pick1_b), ghost1_b)
    finish(FIRST2, 4, faces2, ghost2)
    finish(CROSS2, 4, faces2, cross2, across)
    copy(OP1, 0, op1_half, op1_half, partner).wait_send()
    copy(SRC1, 0, src1_half, src1_half, partner).wait_send()
    copy(SRC2, 0, src2, src2x, mate).wait_send()


def fanout(result_ref, fine_ref, one_ref, two_ref):
    fine_ref[...] = result_ref[0:64]
    one_ref[...] = result_ref[64:72]
    two_ref[...] = result_ref[72:76, 0:32]


def fold(array):
    lead = array.shape[:-2]
    shaped = array.reshape(lead + (array.shape[-2], 16, 128))
    return jnp.swapaxes(shaped, -3, -2).reshape(lead + (16 * array.shape[-2], 128))


def on_device(
    source, operator, prolong, columns, slots, aggregates, sends,
    prolong_one, columns_one, slots_one, aggregates_one, sends_one, columns_two, sends_two,
):
    vmem = pl.BlockSpec(memory_space=pltpu.VMEM)
    landing = [
        ((64, 128), F32), ((28, 64, 128), F32), ((4, 64, 128), F32), ((7, 2048), jnp.int32), ((7, 2048), jnp.int32),
        ((16, 128), jnp.int32), ((16, 128), jnp.int32), ((4, 4, 512), F32), ((7, 512), jnp.int32),
        ((7, 512), jnp.int32), ((4, 128), jnp.int32), ((3, 128), jnp.int32), ((7, 128), jnp.int32),
        ((160,), jnp.int32),
    ]
    scratch = landing + [
        ((128, 128), jnp.int32), ((14, 8, 128), jnp.int32), ((14, 8, 128), jnp.int32),
        ((112, 2, 8, 128), F32), ((4, 2, 8, 128), F32), ((4, 2, 8, 128), F32), ((4, 2, 8, 128), F32),
        ((16, 2, 8, 128), F32), ((4, 14, 8, 128), F32), ((1792, 128), F32),
        ((14, 16, 8, 128), F32), ((1792, 128), F32), ((224, 2048), BF16), ((256, 2048), BF16),
        ((64, 128), F32), ((8, 2048), F32),
        ((4, 4, 4, 128), F32), ((4, 4, 4, 128), F32), ((256, 128), F32),
        ((4, 4, 4, 128), F32), ((4, 4, 4, 128), F32), ((256, 128), F32),
        ((448, 128), F32), ((4, 4, 128), F32), ((32, 128), jnp.int32), ((32, 128), jnp.int32),
        ((64, 128), F32), ((16, 128), F32), ((4, 32, 128), F32), ((16, 32, 128), F32),
        ((7, 16, 4, 128), F32), ((112, 4, 128), F32), ((224, 512), BF16), ((128, 512), BF16),
        ((16, 128), F32), ((8, 512), F32), ((16, 128), F32), ((8, 128), jnp.int32),
        ((3, 16, 128), F32), ((3, 4, 128), F32), ((3, 4, 128), F32),
        ((4, 16, 128), F32), ((4, 4, 128), F32), ((4, 4, 128), F32),
        ((112, 128), F32), ((112, 128), F32), ((8, 128), F32), ((8, 128), F32),
        ((2, 4, 128), F32), ((4, 4, 128), F32), ((4, 4, 128), F32), ((256, 256), F32), ((512, 256), BF16),
    ]
    result = pl.pallas_call(
        kernel,
        out_shape=jax.ShapeDtypeStruct((80, 128), F32),
        in_specs=[pl.BlockSpec(memory_space=pl.ANY)] * 14,
        out_specs=vmem,
        scratch_shapes=[pltpu.VMEM(shape, kind) for shape, kind in scratch]
        + [pltpu.SemaphoreType.DMA(shape) for shape in ((14,), (12, 4), (12, 4))],
        compiler_params=pltpu.CompilerParams(
            collective_id=0, has_side_effects=True, vmem_limit_bytes=60 << 20
        ),
        name="descend",
    )(
        fold(source), fold(operator).reshape(28, 64, 128), fold(prolong), columns, slots,
        aggregates.reshape(16, 128), sends.reshape(16, 128),
        prolong_one, columns_one, slots_one, aggregates_one.reshape(4, 128), sends_one.reshape(3, 128),
        columns_two, sends_two,
    )
    shares = pl.pallas_call(
        fanout,
        out_shape=[jax.ShapeDtypeStruct(shape, F32) for shape in ((64, 128), (8, 128), (4, 32))],
        in_specs=[vmem],
        out_specs=[vmem] * 3,
        name="fanout",
    )(result)

    def unfold(rows):
        return rows.reshape(-1, 4, 128).swapaxes(0, 1).reshape(4, -1)

    return unfold(shares[0]), unfold(shares[1]), shares[2]


def solution(mesh):
    both = ("sub", "slab")
    flat = P(both)
    rows = P(None, both)
    blocks = P(None, None, both)
    placed = (
        rows, P(None, None, None, both), blocks, rows, rows, flat, flat,
        blocks, rows, rows, flat, flat, rows, flat,
    )
    return jax.shard_map(
        on_device, mesh=mesh, in_specs=placed, out_specs=(rows, rows, rows), check_vma=False
    )
```
